128 devices in a mesh: outer: 4 (over z), inner: 32 (over x, y, core).
Axes of the slice: x: 4, y: 4, z: 4, core: 2. Of those that a mesh axis runs over, the one named last changes fastest.
Arguments:
- left_four: float32 [524288, 128], P(('outer', 'inner')), may hold values from -6 to 6
- left_three: float32 [524288, 128], P(('outer', 'inner')), may hold values from -6 to 6
- left_two: float32 [524288, 128], P(('outer', 'inner')), may hold values from -6 to 6
- left_one: float32 [524288, 128], P(('outer', 'inner')), may hold values from -6 to 6
- right_four: float32 [524288, 128], P(('outer', 'inner')), may hold values from -0.0008544922 to 0.0008544922
- right_three: float32 [524288, 128], P(('outer', 'inner')), may hold values from -0.00061035156 to 0.00061035156
- right_two: float32 [524288, 128], P(('outer', 'inner')), may hold values from -0.0004272461 to 0.0004272461
- right_one: float32 [524288, 128], P(('outer', 'inner')), may hold values from -0.00030517578 to 0.00030517578
- loads: float32 [524288, 128], P(('outer', 'inner')), may hold values from -6 to 6
Outputs:
- solution: float32 [524288, 128], P(('outer', 'inner'))
The draws below stay inside these ranges and needn't reach their ends.
All inputs are finite; a program needn't handle non-finite values.
Results may differ from the reference program's by a relative error of at most 0.0003.
Values sent between devices are 32-bit elements; how exact they have to be, the bound alone decides.
A program may use at most 128 MiB of HBM per device.

```python
import jax
import jax.numpy as jnp
from jax import lax

RANK = 128
ORDER = 524288


def steps_of(own_key, dims, cuts, least, top_value):
    loudness, own = 1.0, jax.random.fold_in(own_key, 6)
    for axis_at, shards_of in cuts:
        heights = jnp.exp(jax.random.uniform(jax.random.fold_in(own, axis_at), (shards_of,), jnp.float32, least / len(cuts), top_value / len(cuts)))
        loudness = loudness * jnp.repeat(heights, dims[axis_at] // shards_of).reshape([-1 if axis == axis_at else 1 for axis in range(len(dims))])
    return loudness


def gaussian(own_key, shape, scale, most, cuts=(), kind=jnp.bfloat16):
    array = jax.random.normal(own_key, shape, jnp.float32) * scale
    if len(cuts) > 0:
        array = steps_of(own_key, shape, cuts, -0.22, 0.18) * array
    return jnp.clip(array, min=-most, max=most).astype(kind)


def setup_inputs(seed: int = 0) -> dict:
    key_list = jax.random.split(jax.random.key(seed), 10)
    left_four = gaussian(key_list[0], (ORDER, RANK), 1.0, 6.0, ((0, 128),), jnp.float32)
    left_three = gaussian(key_list[1], (ORDER, RANK), 1.0, 6.0, ((0, 128),), jnp.float32)
    left_two = gaussian(key_list[2], (ORDER, RANK), 1.0, 6.0, ((0, 128),), jnp.float32)
    left_one = gaussian(key_list[3], (ORDER, RANK), 1.0, 6.0, ((0, 128),), jnp.float32)
    right_four = gaussian(key_list[4], (ORDER, RANK), (1600 * ORDER // 16) ** -0.5, 0.0008544922, ((0, 128),), jnp.float32)
    right_three = gaussian(key_list[5], (ORDER, RANK), (1600 * ORDER // 8) ** -0.5, 0.00061035156, ((0, 128),), jnp.float32)
    right_two = gaussian(key_list[6], (ORDER, RANK), (1600 * ORDER // 4) ** -0.5, 0.0004272461, ((0, 128),), jnp.float32)
    right_one = gaussian(key_list[7], (ORDER, RANK), (1600 * ORDER // 2) ** -0.5, 0.00030517578, ((0, 128),), jnp.float32)
    loads = gaussian(key_list[8], (ORDER, RANK), 1.0, 6.0, ((0, 128),), jnp.float32)
    return dict(left_four=left_four, left_three=left_three, left_two=left_two, left_one=left_one, right_four=right_four, right_three=right_three, right_two=right_two, right_one=right_one, loads=loads)


highest = lax.Precision.HIGHEST

def solve_level(basis, right_basis, carried, level_number):
    groups = 2 ** level_number
    width = basis.shape[1]
    columns = carried.shape[1]
    stacked = jnp.concatenate([basis, carried], axis=1).reshape(groups, -1, width + columns)
    rights = right_basis.reshape(groups, -1, width)
    products = jnp.einsum('gnk,gnc->gkc', rights, stacked, precision=highest)
    paired = products.reshape(groups // 2, 2, width, width + columns)
    couplings = paired[:, :, :, :width]
    weights = paired[:, :, :, width:]
    identity = jnp.broadcast_to(jnp.eye(width, dtype=products.dtype), (groups // 2, width, width))
    upper = jnp.concatenate([identity, couplings[:, 1]], axis=2)
    lower = jnp.concatenate([couplings[:, 0], identity], axis=2)
    system = jnp.concatenate([upper, lower], axis=1)
    targets = jnp.concatenate([weights[:, 1], weights[:, 0]], axis=1)
    solved = jnp.linalg.solve(system, targets).reshape(groups, width, columns)
    bases = basis.reshape(groups, -1, width)
    update = jnp.einsum('gnk,gkc->gnc', bases, solved, precision=highest)
    return (stacked[:, :, width:] - update).reshape(-1, columns)

def reference(left_four, left_three, left_two, left_one, right_four, right_three, right_two, right_one, loads):
    width = left_four.shape[1]
    basis = left_four
    carried = jnp.concatenate([left_three, left_two, left_one, loads], axis=1)
    updated = carried
    for level_number, right_basis in ((4, right_four), (3, right_three), (2, right_two), (1, right_one)):
        updated = solve_level(basis, right_basis, carried, level_number)
        basis = updated[:, :width]
        carried = updated[:, width:]
    return updated
```

```python
import functools

import jax
import jax.numpy as jnp
from jax import lax
from jax.experimental import pallas as pl
from jax.experimental.pallas import tpu as pltpu
from jax.sharding import PartitionSpec as P

W = 128
HIGH = lax.Precision.HIGH
HIGHEST = lax.Precision.HIGHEST
MESH = pl.DeviceIdType.MESH


def dot(a, b, precision=HIGHEST):
    return jnp.dot(a, b, precision=precision, preferred_element_type=jnp.float32)


def split(v):
    high = v.astype(jnp.bfloat16)
    low = (v - high.astype(jnp.float32)).astype(jnp.bfloat16)
    return high, low


def products_kernel(l4, l3, l2, l1, x, r4, r3, r2, r1, out, acc):
    step = pl.program_id(0)

    @pl.when(step == 0)
    def _():
        acc[...] = jnp.zeros_like(acc)

    rights = jnp.concatenate([r4[...], r3[...], r2[...], r1[...]], axis=1)
    r_high, r_low = split(rights)
    a_high, a_low = [], []
    for ref in (l4, l3, l2, l1, x):
        high, low = split(ref[...].T)
        a_high.append(high)
        a_low.append(low)
    a_high = jnp.concatenate(a_high, axis=0)
    a_low = jnp.concatenate(a_low, axis=0)
    one = functools.partial(jnp.dot, preferred_element_type=jnp.float32)
    acc[...] += one(a_high, r_high) + one(a_high, r_low) + one(a_low, r_high)

    @pl.when(step == pl.num_programs(0) - 1)
    def _():
        for core in range(2):
            for y in range(4):
                piece = y * 2 + core
                for block in range(5):
                    out[core, y, 16 * block : 16 * block + 16, :] = acc[
                        W * block + 16 * piece : W * block + 16 * piece + 16, :
                    ]


def products(lefts, rights, tile=512):
    rows = lefts[0].shape[0]
    spec = pl.BlockSpec((tile, W), lambda i: (i, 0))
    return pl.pallas_call(
        products_kernel,
        grid=(rows // tile,),
        out_shape=jax.ShapeDtypeStruct((2, 4, 80, 512), jnp.float32),
        in_specs=[spec] * 9,
        out_specs=pl.BlockSpec((2, 4, 80, 512), lambda i: (0, 0, 0, 0)),
        scratch_shapes=[pltpu.VMEM((640, 512), jnp.float32)],
        name="products",
    )(*lefts, *rights)


def inverse(matrix):
    tiles = [matrix[8 * i : 8 * i + 8, :] for i in range(16)]
    lane = lax.broadcasted_iota(jnp.int32, (8, W), 1)
    sub = lax.broadcasted_iota(jnp.int32, (8, W), 0)

    def block_step(block, tiles):
        first = block * 8
        in_block = (lane >= first) & (lane < first + 8)
        on_diag = lane == first + sub

        def column(tile, i):
            index = jnp.zeros((8, W), jnp.int32) + (first + i)
            return jnp.take_along_axis(tile, index, axis=1, mode="promise_in_bounds")

        pivot_tile = tiles[0]
        cols = [column(pivot_tile, i) for i in range(8)]
        panel = jnp.where(in_block, jnp.where(on_diag, 1.0, 0.0), pivot_tile)
        for i in range(8):
            inv = 1.0 / jnp.broadcast_to(cols[i][i : i + 1, :], (8, W))
            here = sub == i
            row = jnp.broadcast_to(panel[i : i + 1, :], (8, W)) * inv
            panel = jnp.where(here, row, panel - cols[i] * row)
            for j in range(i + 1, 8):
                row = jnp.broadcast_to(cols[j][i : i + 1, :], (8, W)) * inv
                cols[j] = jnp.where(here, row, cols[j] - cols[i] * row)
        rows = [jnp.broadcast_to(panel[i : i + 1, :], (8, W)) for i in range(8)]
        updated = []
        for tile in tiles[1:]:
            total = column(tile, 0) * rows[0]
            for i in range(1, 8):
                total = total + column(tile, i) * rows[i]
            updated.append(jnp.where(in_block, 0.0, tile) - total)
        return tuple(updated) + (panel,)

    tiles = lax.fori_loop(0, 16, block_step, tuple(tiles))
    return jnp.concatenate(tiles, axis=0)


def tree_kernel(h, coef, half, rx1, rx2, own, rest, gat, gatx, us, sems):
    z = lax.axis_index("outer")
    inner = lax.axis_index("inner")
    x = inner // 8
    y = lax.rem(inner, 8) // 2
    core = lax.rem(inner, 2)
    mine = y * 2 + core

    def device(dz_to, x_to, dy, dc):
        y_to = lax.rem(y + dy, 4)
        c_to = lax.rem(core + dc, 2)
        return (dz_to, x_to * 8 + y_to * 2 + c_to)

    partners = (
        (z, x + 1 - 2 * lax.rem(x, 2)),
        (z, lax.rem(x + 2, 4)),
        (z + 1 - 2 * lax.rem(z, 2), x),
        (lax.rem(z + 2, 4), x),
    )
    around = [(dy, dc) for dy in range(4) for dc in range(2)]
    peers = [(z, x, dy, dc) for dy, dc in around if (dy, dc) != (0, 0)]
    for zp, xp in partners:
        peers += [(zp, xp, dy, dc) for dy, dc in around]
    barrier = pltpu.get_barrier_semaphore()
    for peer in peers:
        pl.semaphore_signal(barrier, inc=1, device_id=device(*peer), device_id_type=MESH)
    pl.semaphore_wait(barrier, len(peers))

    count = [0]
    started = []

    def send(src, dst, to):
        k = count[0]
        count[0] += 1
        copy = pltpu.make_async_remote_copy(
            src_ref=src, dst_ref=dst, send_sem=sems.at[0, k], recv_sem=sems.at[1, k],
            device_id=device(*to), device_id_type=MESH,
        )
        copy.start()
        started.append(copy)
        return copy

    def receive(copies):
        for copy in copies:
            copy.wait_recv()

    first = send(h.at[1 - core], rx1, (z, x, 0, 1))
    receive([first])
    half[...] = h[core] + rx1[...]
    copies = []
    for dy in (1, 2, 3):
        copies.append(send(half.at[lax.rem(y + dy, 4)], rx2.at[dy - 1], (z, x, dy, 0)))
    receive(copies)
    own[0][...] = half[y] + rx2[0] + rx2[1] + rx2[2]

    eye = jnp.where(
        lax.broadcasted_iota(jnp.int32, (W, W), 0) == lax.broadcasted_iota(jnp.int32, (W, W), 1), 1.0, 0.0
    )
    spread = []
    for level in range(4):
        lanes = 4 - level
        rows = 16 * lanes
        zp, xp = partners[level]
        mat, gather = own[level], gat[level]
        at = pl.ds(pl.multiple_of(mine * 16, 16), 16)
        pivots, others, x_rows = [], [], []
        for side in range(2):
            zt, xt = ((z, x), (zp, xp))[side]
            for dy, dc in around:
                if side == 0 and (dy, dc) == (0, 0):
                    continue
                to = (zt, xt, dy, dc)
                pivots.append(send(mat.at[0:16, 0:W], gather.at[side, at, 0:W], to))
                if level == 3:
                    x_rows.append(send(mat.at[16:32, :], gatx.at[side, at, :], to))
        if level < 3:
            partner_copy = send(mat.at[16 : 16 + rows, :], rest[level], (zp, xp, 0, 0))
            for side in range(2):
                zt, xt = ((z, x), (zp, xp))[side]
                for dy, dc in around:
                    if side == 0 and (dy, dc) == (0, 0):
                        continue
                    to = (zt, xt, dy, dc)
                    others.append(send(mat.at[0:16, W:], gather.at[side, at, W:], to))
        gather[0, at, :] = mat[0:16, :]
        if level == 3:
            gatx[0, at, :] = mat[16:32, :]
        receive(pivots)
        p_own = gather[0, :, 0:W]
        p_sib = gather[1, :, 0:W]
        inv = inverse(eye - dot(p_own, p_sib))
        if level < 3:
            receive([partner_copy])
            w_own = mat[16 : 16 + rows, 0:W]
            w_sib = rest[level][:, 0:W]
        else:
            receive(x_rows)
            w_own = gatx[0]
            w_sib = gatx[1]
        u_own = dot(w_sib - dot(w_own, p_sib), inv)
        if level == 3:
            y_one = u_own
            break
        us[level][mine] = u_own
        copies = []
        for dy, dc in around[1:]:
            copies.append(send(us[level].at[mine], us[level].at[mine], (z, x, dy, dc)))
        spread.append(copies)
        u_sib = w_own - dot(u_own, p_own)
        receive(others)
        own[level + 1][...] = (
            mat[16 : 16 + rows, W:]
            + rest[level][:, W:]
            - dot(u_own, gather[0, :, W:])
            - dot(u_sib, gather[1, :, W:])
        )

    for copies in spread:
        receive(copies)
    u4 = [us[0][:, 16 * b : 16 * b + 16, :].reshape(W, W) for b in range(4)]
    u3 = [us[1][:, 16 * b : 16 * b + 16, :].reshape(W, W) for b in range(3)]
    u2 = [us[2][:, 16 * b : 16 * b + 16, :].reshape(W, W) for b in range(2)]
    y_two = u2[1] - dot(y_one, u2[0])
    y_three = u3[2] - dot(y_one, u3[1]) - dot(y_two, u3[0])
    y_four = u4[3] - dot(y_one, u4[2]) - dot(y_two, u4[1]) - dot(y_three, u4[0])
    coef[0] = y_four
    coef[1] = y_three
    coef[2] = y_two
    coef[3] = y_one
    for copy in started:
        copy.wait_send()


def tree(sums):
    f32 = jnp.float32
    vmem = pl.BlockSpec(memory_space=pltpu.VMEM)
    n_copies = 4 + 4 * 15 + 15 + 3 + 3 * 15 + 3 * 7
    return pl.pallas_call(
        tree_kernel,
        out_shape=jax.ShapeDtypeStruct((4, W, W), f32),
        in_specs=[vmem],
        out_specs=vmem,
        scratch_shapes=[
            pltpu.VMEM((4, 80, 512), f32),
            pltpu.VMEM((4, 80, 512), f32),
            pltpu.VMEM((3, 80, 512), f32),
            [pltpu.VMEM((16 * (5 - k), W * (4 - k)), f32) for k in range(4)],
            [pltpu.VMEM((16 * (4 - k), W * (4 - k)), f32) for k in range(3)],
            [pltpu.VMEM((2, W, W * (4 - k)), f32) for k in range(4)],
            pltpu.VMEM((2, W, W), f32),
            [pltpu.VMEM((8, 16 * (4 - k), W), f32) for k in range(3)],
            pltpu.SemaphoreType.DMA((2, n_copies)),
        ],
        compiler_params=pltpu.CompilerParams(collective_id=0, has_side_effects=True),
        name="tree",
    )(sums)


def update_kernel(l4, l3, l2, l1, x, coef, out):
    total = x[...]
    for index, ref in enumerate((l4, l3, l2, l1)):
        total = total - lax.dot_general(
            ref[...], coef[index], (((1,), (1,)), ((), ())), precision=HIGH, preferred_element_type=jnp.float32
        )
    out[...] = total


def update(lefts, coef, tile=512):
    rows = lefts[0].shape[0]
    spec = pl.BlockSpec((tile, W), lambda i: (i, 0))
    return pl.pallas_call(
        update_kernel,
        grid=(rows // tile,),
        out_shape=jax.ShapeDtypeStruct((rows, W), jnp.float32),
        in_specs=[spec] * 5 + [pl.BlockSpec((4, W, W), lambda i: (0, 0, 0))],
        out_specs=spec,
        name="update",
    )(*lefts, coef)


def body(l4, l3, l2, l1, r4, r3, r2, r1, x):
    lefts = (l4, l3, l2, l1, x)
    sums = products(lefts, (r4, r3, r2, r1))
    coef = tree(sums)
    return update(lefts, coef)


def solution(mesh):
    spec = P(("outer", "inner"), None)
    return jax.shard_map(body, mesh=mesh, in_specs=(spec,) * 9, out_specs=spec, check_vma=False)
```

```python
import functools

import jax
import jax.numpy as jnp
from jax import lax
from jax.experimental import pallas as pl
from jax.experimental.pallas import tpu as pltpu
from jax.sharding import PartitionSpec as P

W = 128
HIGH = lax.Precision.HIGH
HIGHEST = lax.Precision.HIGHEST
MESH = pl.DeviceIdType.MESH


def dot(a, b, precision=HIGHEST):
    return jnp.dot(a, b, precision=precision, preferred_element_type=jnp.float32)


def split(v):
    high = v.astype(jnp.bfloat16)
    low = (v - high.astype(jnp.float32)).astype(jnp.bfloat16)
    return high, low


def inverse(matrix, between):
    tiles = [matrix[8 * i : 8 * i + 8, :] for i in range(16)]
    lane = lax.broadcasted_iota(jnp.int32, (8, W), 1)
    sub = lax.broadcasted_iota(jnp.int32, (8, W), 0)

    def block_step(block, tiles):
        first = block * 8
        in_block = (lane >= first) & (lane < first + 8)
        on_diag = lane == first + sub

        def column(tile, i):
            index = jnp.zeros((8, W), jnp.int32) + (first + i)
            return jnp.take_along_axis(tile, index, axis=1, mode="promise_in_bounds")

        pivot_tile = tiles[0]
        cols = [column(pivot_tile, i) for i in range(8)]
        panel = jnp.where(in_block, jnp.where(on_diag, 1.0, 0.0), pivot_tile)
        for i in range(8):
            inv = 1.0 / jnp.broadcast_to(cols[i][i : i + 1, :], (8, W))
            here = sub == i
            row = jnp.broadcast_to(panel[i : i + 1, :], (8, W)) * inv
            panel = jnp.where(here, row, panel - cols[i] * row)
            for j in range(i + 1, 8):
                row = jnp.broadcast_to(cols[j][i : i + 1, :], (8, W)) * inv
                cols[j] = jnp.where(here, row, cols[j] - cols[i] * row)
        rows = [jnp.broadcast_to(panel[i : i + 1, :], (8, W)) for i in range(8)]
        updated = []
        for tile in tiles[1:]:
            total = column(tile, 0) * rows[0]
            for i in range(1, 8):
                total = total + column(tile, i) * rows[i]
            updated.append(jnp.where(in_block, 0.0, tile) - total)
        return tuple(updated) + (panel,)

    tiles = lax.fori_loop(0, 8, block_step, tuple(tiles))
    between()
    tiles = lax.fori_loop(8, 16, block_step, tiles)
    return jnp.concatenate(tiles, axis=0)


ROWS = 4096
CHUNK = 512
CHUNKS = ROWS // CHUNK


def solve_kernel(
    l4, l3, l2, l1, x_in, r4, r3, r2, r1, out, a_buf, r_buf, r_high, r_low, h, rx1, half, rx2,
    own, rest, gat, gatx, us, load_sems, out_sems, sems,
):
    z = lax.axis_index("outer")
    inner = lax.axis_index("inner")
    x = inner // 8
    y = lax.rem(inner, 8) // 2
    core = lax.rem(inner, 2)
    mine = core * 4 + y

    def device(z_to, x_to, dy, dc):
        y_to = lax.rem(y + dy, 4)
        c_to = lax.rem(core + dc, 2)
        return (z_to, x_to * 8 + y_to * 2 + c_to)

    partners = (
        (z, x + 1 - 2 * lax.rem(x, 2)),
        (z, lax.rem(x + 2, 4)),
        (z + 1 - 2 * lax.rem(z, 2), x),
        (lax.rem(z + 2, 4), x),
    )
    around = [(dy, dc) for dc in range(2) for dy in range(4)]
    peers = [(z, x, dy, dc) for dy, dc in around[1:]]
    for zp, xp in partners:
        peers += [(zp, xp, dy, dc) for dy, dc in around]
    barrier = pltpu.get_barrier_semaphore()
    for peer in peers:
        pl.semaphore_signal(barrier, inc=1, device_id=device(*peer), device_id_type=MESH)

    def load(source, target, k):
        loads = []
        for c in range(CHUNKS):
            rows = pl.ds(c * CHUNK, CHUNK)
            loads.append(pltpu.make_async_copy(source.at[rows, :], target.at[rows, :], load_sems.at[k, c]))
        return loads

    rights = [load(ref, r_buf.at[i], 5 + i) for i, ref in enumerate((r4, r3, r2, r1))]
    lefts = [load(ref, a_buf.at[i], i) for i, ref in enumerate((l4, l3, l2, l1, x_in))]
    for c in range(CHUNKS):
        for loads in rights + lefts[:1]:
            loads[c].start()
    for loads in lefts[1:]:
        for copy in loads:
            copy.start()

    count = [0]
    started = []

    def send(src, dst, to):
        k = count[0]
        count[0] += 1
        copy = pltpu.make_async_remote_copy(
            src_ref=src, dst_ref=dst, send_sem=sems.at[0, k], recv_sem=sems.at[1, k],
            device_id=device(*to), device_id_type=MESH,
        )
        copy.start()
        started.append(copy)
        return copy

    def receive(copies):
        for copy in copies:
            copy.wait_recv()

    one = functools.partial(jnp.dot, preferred_element_type=jnp.float32)

    def product(group, start, size):
        rows = pl.ds(start, size)
        high, low = split(a_buf[group, rows, :].T)
        both = one(jnp.concatenate([high, low], axis=0), r_high[rows, :])
        total = both[:W] + both[W:] + one(high, r_low[rows, :])
        return total.reshape(2, 4, 16, 512)

    mine_rows = pl.ds(pl.multiple_of(mine * 16, 16), 16)
    core_rows = pl.ds(pl.multiple_of(core * 64, 64), 64)
    pivots = [[] for _ in range(4)]
    others = [[] for _ in range(4)]
    nexts = [[] for _ in range(4)]
    rests = [[] for _ in range(4)]

    def send_pivot_rows(level):
        mat, gather = own[level], gat[level]
        zp, xp = partners[level]
        targets = [(z, x, dy, dc) for dy, dc in around[1:]] + [(zp, xp, dy, dc) for dy, dc in around]
        for k, to in enumerate(targets):
            side = 0 if k < 7 else 1
            pivots[level].append(send(mat.at[0:16, 0:W], gather.at[side, mine_rows, 0:W], to))
        gather[0, mine_rows, :] = mat[0:16, :]

    def send_side_rows(level):
        zp, xp = partners[level]
        targets = [(z, x, dy, 0) for dy in (1, 2, 3)] + [(zp, xp, dy, 0) for dy in range(4)]
        for k, to in enumerate(targets):
            side = 0 if k < 3 else 1
            if level < 3:
                copy = send(own[level].at[0:16, W:], gat[level].at[side, mine_rows, W:], to)
            else:
                copy = send(own[3].at[16:32, :], gatx.at[side, mine_rows, :], to)
            others[level].append(copy)
        if level == 3:
            gatx[0, mine_rows, :] = own[3][16:32, :]

    first = [None] * 5
    second = [None] * 5

    def sum_cores(group):
        first[group] = send(h[group].at[1 - core], rx1[group], (z, x, 0, 1))

    def sum_chips(group):
        receive([first[group]])
        half[group][...] = h[group][core] + rx1[group][...]
        second[group] = [
            send(half[group].at[lax.rem(y + dy, 4)], rx2[group].at[dy - 1], (z, x, dy, 0)) for dy in (1, 2, 3)
        ]

    def finish_sum(group):
        receive(second[group])
        rows = slice(16 * group, 16 * group + 16)
        own[0][rows, :] = half[group][y] + rx2[group][0] + rx2[group][1] + rx2[group][2]
        if group == 0:
            send_pivot_rows(0)
            send_side_rows(0)
        else:
            target = rest[0].at[16 * (group - 1) : 16 * group, :]
            copy = send(own[0].at[rows, :], target, partners[0] + (0, 0))
            (nexts if group == 1 else rests)[0].append(copy)

    for c in range(CHUNKS):
        rows = pl.ds(c * CHUNK, CHUNK)
        for i, loads in enumerate(rights):
            loads[c].wait()
            high, low = split(r_buf[i, rows, :])
            r_high[rows, W * i : W * i + W] = high
            r_low[rows, W * i : W * i + W] = low
        lefts[0][c].wait()
        part = product(0, c * CHUNK, CHUNK)
        if c == 0:
            h[0][...] = part
        else:
            h[0][...] += part
    pl.semaphore_wait(barrier, len(peers))
    sum_cores(0)
    for group in range(1, 5):
        for part in range(2):
            for c in range(CHUNKS // 2):
                lefts[group][part * (CHUNKS // 2) + c].wait()
            value = product(group, part * (ROWS // 2), ROWS // 2)
            if part == 0:
                h[group][...] = value
                sum_chips(group - 1)
                if group > 1:
                    finish_sum(group - 2)
            else:
                h[group][...] += value
        sum_cores(group)

    eye = jnp.where(
        lax.broadcasted_iota(jnp.int32, (W, W), 0) == lax.broadcasted_iota(jnp.int32, (W, W), 1), 1.0, 0.0
    )
    forwards = []
    spread = [[] for _ in range(3)]

    def forward(ref):
        forwards.append(send(ref, ref, (z, x, 0, 1)))
        return forwards[-1]

    u_forwards = []
    for level in range(4):
        lanes = 4 - level
        mat, gather = own[level], gat[level]
        if level == 0:
            sum_chips(4)
            finish_sum(3)
        receive(pivots[level])
        p_own = gather[0, :, 0:W]
        p_sib = gather[1, :, 0:W]
        side_forward = []

        def between(level=level, gather=gather, side_forward=side_forward):
            receive(others[level])
            if level < 3:
                side_forward.append(forward(gather.at[:, core_rows, W:]))
            else:
                side_forward.append(forward(gatx.at[:, core_rows, :]))
            if level > 0:
                receive(spread[level - 1])
                u_forwards.append(forward(us[level - 1].at[pl.ds(core * 4, 4)]))

        inv = inverse(eye - dot(p_own, p_sib), between)
        if level == 3:
            receive(side_forward)
            y_one = dot(gatx[1] - dot(gatx[0], p_sib), inv)
            break
        if level == 0:
            finish_sum(4)
        for stage in range(2):
            low, top = (16, 32) if stage == 0 else (32, 16 + 16 * lanes)
            receive((nexts if stage == 0 else rests)[level])
            w_own = mat[low:top, 0:W]
            w_sib = rest[level][low - 16 : top - 16, 0:W]
            u_own = dot(w_sib - dot(w_own, p_sib), inv)
            u_sib = w_own - dot(u_own, p_own)
            us[level][mine, low - 16 : top - 16, :] = u_own
            if stage == 0:
                receive(side_forward)
            own[level + 1][low - 16 : top - 16, :] = (
                mat[low:top, W:]
                + rest[level][low - 16 : top - 16, W:]
                - dot(u_own, gather[0, :, W:])
                - dot(u_sib, gather[1, :, W:])
            )
            if stage == 0:
                send_pivot_rows(level + 1)
                if level < 2:
                    send_side_rows(level + 1)
        partner = partners[level + 1] + (0, 0)
        if level < 2:
            nexts[level + 1].append(send(own[level + 1].at[16:32, :], rest[level + 1].at[0:16, :], partner))
            rests[level + 1].append(send(own[level + 1].at[32:, :], rest[level + 1].at[16:, :], partner))
        else:
            send_side_rows(3)
        for dy in (1, 2, 3):
            spread[level].append(send(us[level].at[mine], us[level].at[mine], (z, x, dy, 0)))

    receive(u_forwards)
    u4 = [us[0][:, 16 * b : 16 * b + 16, :].reshape(W, W) for b in range(4)]
    u3 = [us[1][:, 16 * b : 16 * b + 16, :].reshape(W, W) for b in range(3)]
    u2 = [us[2][:, 16 * b : 16 * b + 16, :].reshape(W, W) for b in range(2)]
    y_two = u2[1] - dot(y_one, u2[0])
    y_three = u3[2] - dot(y_one, u3[1]) - dot(y_two, u3[0])
    y_four = u4[3] - dot(y_one, u4[2]) - dot(y_two, u4[1]) - dot(y_three, u4[0])

    y_high, y_low = split(jnp.concatenate([y_four.T, y_three.T, y_two.T, y_one.T], axis=0))
    y_both = jnp.concatenate([y_high, y_low], axis=1)
    stores = []
    for c in range(CHUNKS):
        rows = pl.ds(c * CHUNK, CHUNK)
        basis = jnp.concatenate([a_buf[i, rows, :] for i in range(4)], axis=1)
        high, low = split(basis)
        both = one(high, y_both)
        a_buf[4, rows, :] = a_buf[4, rows, :] - (both[:, :W] + both[:, W:] + one(low, y_high))
        stores.append(pltpu.make_async_copy(a_buf.at[4, rows, :], out.at[rows, :], out_sems.at[c]))
        stores[-1].start()
    for copy in stores:
        copy.wait()
    for copy in started:
        copy.wait_send()


def body(l4, l3, l2, l1, r4, r3, r2, r1, x):
    f32, bf16 = jnp.float32, jnp.bfloat16
    hbm = pl.BlockSpec(memory_space=pl.ANY)
    n_copies = 5 * 4 + 4 + 4 * 15 + 4 * 7 + 2 * 2 + 4 + 3 * 3 + 3
    return pl.pallas_call(
        solve_kernel,
        out_shape=jax.ShapeDtypeStruct((ROWS, W), f32),
        in_specs=[hbm] * 9,
        out_specs=hbm,
        scratch_shapes=[
            pltpu.VMEM((5, ROWS, W), f32),
            pltpu.VMEM((4, ROWS, W), f32),
            pltpu.VMEM((ROWS, 512), bf16),
            pltpu.VMEM((ROWS, 512), bf16),
            [pltpu.VMEM((2, 4, 16, 512), f32) for _ in range(5)],
            [pltpu.VMEM((4, 16, 512), f32) for _ in range(5)],
            [pltpu.VMEM((4, 16, 512), f32) for _ in range(5)],
            [pltpu.VMEM((3, 16, 512), f32) for _ in range(5)],
            [pltpu.VMEM((16 * (5 - k), W * (4 - k)), f32) for k in range(4)],
            [pltpu.VMEM((16 * (4 - k), W * (4 - k)), f32) for k in range(3)],
            [pltpu.VMEM((2, W, W * (4 - k)), f32) for k in range(4)],
            pltpu.VMEM((2, W, W), f32),
            [pltpu.VMEM((8, 16 * (4 - k), W), f32) for k in range(3)],
            pltpu.SemaphoreType.DMA((9, CHUNKS)),
            pltpu.SemaphoreType.DMA((CHUNKS,)),
            pltpu.SemaphoreType.DMA((2, n_copies)),
        ],
        compiler_params=pltpu.CompilerParams(
            collective_id=0, has_side_effects=True, vmem_limit_bytes=60 * 1024 * 1024
        ),
        name="solve",
    )(l4, l3, l2, l1, x, r4, r3, r2, r1)


def solution(mesh):
    spec = P(("outer", "inner"), None)
    return jax.shard_map(body, mesh=mesh, in_specs=(spec,) * 9, out_specs=spec, check_vma=False)
```

```python
import functools

import jax
import jax.numpy as jnp
from jax import lax
from jax.experimental import pallas as pl
from jax.experimental.pallas import tpu as pltpu
from jax.sharding import PartitionSpec as P

W = 128
HALF = 64
ROWS = 4096
CHUNK = 1024
CHUNKS = ROWS // CHUNK
HIGH = lax.Precision.HIGH
HIGHEST = lax.Precision.HIGHEST
MESH = pl.DeviceIdType.MESH


def dot(a, b, precision=HIGHEST):
    return jnp.dot(a, b, precision=precision, preferred_element_type=jnp.float32)


def split(v):
    high = v.astype(jnp.bfloat16)
    low = (v - high.astype(jnp.float32)).astype(jnp.bfloat16)
    return high, low


def inverse(matrix, between=None):
    lane = lax.broadcasted_iota(jnp.int32, (8, W), 1)
    sub = lax.broadcasted_iota(jnp.int32, (8, W), 0)
    lane_half = lax.broadcasted_iota(jnp.int32, (HALF, W), 1)
    row_whole = lax.broadcasted_iota(jnp.int32, (W, W), 0)

    def column(tile, index):
        return jnp.take_along_axis(tile, jnp.full((8, W), index, jnp.int32), axis=1, mode="promise_in_bounds")

    def spread(tile, i):
        return jnp.broadcast_to(tile[i : i + 1], (8, W))

    def block_step(block, halves):
        start = block * HALF
        panel, rest = halves
        tiles = [panel[8 * i : 8 * i + 8] for i in range(8)]
        for step in range(8):
            begin = start + 8 * step
            inside = (lane >= begin) & (lane < begin + 8)
            cols = [column(tiles[step], begin + i) for i in range(8)]
            pivot = jnp.where(inside, jnp.where(lane == begin + sub, 1.0, 0.0), tiles[step])
            for i in range(0, 8, 2):
                left, right = cols[i], cols[i + 1]
                a, b, c, d = spread(left, i), spread(right, i), spread(left, i + 1), spread(right, i + 1)
                inv = 1.0 / (a * d - b * c)
                at_one, at_two = sub == i, sub == i + 1

                def sweep(tile):
                    one, two = spread(tile, i), spread(tile, i + 1)
                    first = (d * one - b * two) * inv
                    second = (a * two - c * one) * inv
                    other = tile - (left * first + right * second)
                    return jnp.where(at_one, first, jnp.where(at_two, second, other))

                for j in range(i + 2, 8):
                    cols[j] = sweep(cols[j])
                pivot = sweep(pivot)
            rows = [jnp.broadcast_to(pivot[i : i + 1], (8, W)) for i in range(8)]
            for t in range(8):
                if t == step:
                    continue
                terms = [column(tiles[t], begin + i) * rows[i] for i in range(8)]
                while len(terms) > 1:
                    terms = [terms[k] + terms[k + 1] for k in range(0, len(terms), 2)]
                tiles[t] = jnp.where(inside, 0.0, tiles[t]) - terms[0]
            tiles[step] = pivot
        panel = jnp.concatenate(tiles, axis=0)
        tall = jnp.where(
            (row_whole >= start) & (row_whole < start + HALF), jnp.concatenate([panel, panel], axis=0), 0.0
        )
        inside = (lane_half >= start) & (lane_half < start + HALF)
        return jnp.where(inside, 0.0, rest) - dot(rest, tall), panel

    halves = (matrix[:HALF], matrix[HALF:])
    if between is None:
        halves = lax.fori_loop(0, 2, block_step, halves)
    else:
        halves = lax.fori_loop(0, 1, block_step, halves)
        between()
        halves = lax.fori_loop(1, 2, block_step, halves)
    return jnp.concatenate(halves, axis=0)


def solve_kernel(
    l4, l3, l2, l1, x_in, r4, r3, r2, r1, out, a_buf, r_buf, r_high, r_low, acc, h, rx0, rx1, half, rx2,
    own, rest, gat, gatx, us, inv_buf, load_sems, out_sems, sems,
):
    z = lax.axis_index("outer")
    inner = lax.axis_index("inner")
    x = inner // 8
    y = lax.rem(inner, 8) // 2
    core = lax.rem(inner, 2)
    mine = core * 4 + y

    def load(refs, buffer, offset, k):
        chunks = []
        for c in range(CHUNKS):
            rows = pl.ds(c * CHUNK, CHUNK)
            chunks.append([
                pltpu.make_async_copy(ref.at[rows, :], buffer.at[offset + i, rows, :], load_sems.at[k + i, c])
                for i, ref in enumerate(refs)
            ])
        return chunks

    loads = [r + a for r, a in zip(load((r4, r3, r2, r1), r_buf, 0, 0), load((l4, l3), a_buf, 0, 4))]
    late_loads = load((l2, l1, x_in), a_buf, 2, 6)
    for chunk in loads + late_loads:
        for copy in chunk:
            copy.start()

    def device(z_to, x_to, dy, dc):
        y_to = lax.rem(y + dy, 4)
        c_to = lax.rem(core + dc, 2)
        return (z_to, x_to * 8 + y_to * 2 + c_to)

    partners = (
        (z, x + 1 - 2 * lax.rem(x, 2)),
        (z, lax.rem(x + 2, 4)),
        (z + 1 - 2 * lax.rem(z, 2), x),
        (lax.rem(z + 2, 4), x),
    )
    around = [(dy, dc) for dy in (2, 1, 3, 0) for dc in (1, 0)]
    near = [(z, x, dy, dc) for dy, dc in around[:7]]
    far = [[(zp, xp, dy, dc) for dy, dc in around] for zp, xp in partners]
    peers = far[3] + far[1] + far[2] + far[0] + near
    barrier = pltpu.get_barrier_semaphore()
    for peer in peers:
        pl.semaphore_signal(barrier, inc=1, device_id=device(*peer), device_id_type=MESH)

    count = [0]
    started = []

    def send(src, dst, to):
        k = count[0]
        count[0] += 1
        copy = pltpu.make_async_remote_copy(
            src_ref=src, dst_ref=dst, send_sem=sems.at[0, k], recv_sem=sems.at[1, k],
            device_id=device(*to), device_id_type=MESH,
        )
        copy.start()
        started.append(copy)
        return copy

    def receive(copies):
        for copy in copies:
            copy.wait_recv()

    one = functools.partial(jnp.dot, preferred_element_type=jnp.float32)

    def product(blocks, rows, high, low):
        parts = [split(a_buf[i, rows, :].T) for i in blocks]
        a_high = jnp.concatenate([part[0] for part in parts], axis=0)
        a_low = jnp.concatenate([part[1] for part in parts], axis=0)
        return one(a_high, high) + one(a_low, high) + one(a_high, low)

    total = None
    for c in range(CHUNKS):
        rows = pl.ds(c * CHUNK, CHUNK)
        for copy in loads[c]:
            copy.wait()
        high, low = split(jnp.concatenate([r_buf[i, rows, :] for i in range(4)], axis=1))
        r_high[rows, :] = high
        r_low[rows, :] = low
        total = product((0, 1), rows, high, low)
        if c > 0:
            total = acc[0 : 2 * W, :] + total
        if c < CHUNKS - 1:
            acc[0 : 2 * W, :] = total
    h[0][...] = total[:W].reshape(2, 4, 16, 512)
    h[1][...] = total[W:].reshape(2, 4, 16, 512)
    pl.semaphore_wait(barrier, len(peers))

    def late_product(c):
        rows = pl.ds(c * CHUNK, CHUNK)
        for copy in late_loads[c]:
            copy.wait()
        total = product((2, 3, 4), rows, r_high[rows, :], r_low[rows, :])
        if c > 0:
            total = acc[...] + total
        if c < CHUNKS - 1:
            acc[...] = total
        else:
            h[2][...] = total[:W].reshape(2, 4, 16, 512)
            h[3][:, :, 0:16, :] = total[W : 2 * W].reshape(2, 4, 16, 512)
            h[3][:, :, 16:32, :] = total[2 * W :].reshape(2, 4, 16, 512)

    mine_rows = pl.ds(pl.multiple_of(mine * 16, 16), 16)
    pivots = [[] for _ in range(4)]
    others = [[] for _ in range(4)]
    nexts = [[] for _ in range(4)]
    rests = [[] for _ in range(4)]

    def send_pivot_rows(level):
        mat, gather = own[level], gat[level]
        for side, targets in ((1, far[level]), (0, near)):
            for to in targets:
                pivots[level].append(send(mat.at[0:16, 0:W], gather.at[side, mine_rows, 0:W], to))
        gather[0, mine_rows, 0:W] = mat[0:16, 0:W]

    def send_side_rows(level):
        for side, targets in ((1, far[level]), (0, near)):
            for to in targets:
                if level < 2 and to[3] == 1:
                    continue
                if level < 3:
                    copy = send(own[level].at[0:16, W:], gat[level].at[side, mine_rows, W:], to)
                else:
                    copy = send(own[3].at[16:32, :], gatx.at[side, mine_rows, :], to)
                others[level].append(copy)
        if level == 3:
            gatx[0, mine_rows, :] = own[3][16:32, :]
        else:
            gat[level][0, mine_rows, W:] = own[level][0:16, W:]

    first = [None] * 4
    second = [None] * 4

    def send_core(piece):
        low = W if piece == 0 else 0
        first[piece] = send(h[piece].at[1 - core, :, :, low:], rx1[piece], (z, x, 0, 1))

    def sum_cores(piece):
        receive([first[piece]])
        low = W if piece == 0 else 0
        half[piece][...] = h[piece][core, :, :, low:] + rx1[piece][...]

    def send_chips(piece):
        second[piece] = [
            send(half[piece].at[lax.rem(y + dy, 4)], rx2[piece].at[dy - 1], (z, x, dy, 0)) for dy in (2, 1, 3)
        ]

    def sum_chips(piece, rows):
        receive(second[piece])
        low = W if piece == 0 else 0
        own[0][rows, low:] = half[piece][y] + rx2[piece][0] + rx2[piece][1] + rx2[piece][2]

    direct = []
    for k, (_, _, dy, dc) in enumerate(near):
        piece = h[0].at[lax.rem(core + dc, 2), lax.rem(y + dy, 4), :, 0:W]
        direct.append(send(piece, rx0.at[k], (z, x, dy, dc)))
    send_core(0)
    send_core(1)
    late_product(0)
    sum_cores(0)
    send_chips(0)
    late_product(1)
    receive(direct)
    couplings = h[0][core, y, :, 0:W]
    for k in range(7):
        couplings = couplings + rx0[k]
    own[0][0:16, 0:W] = couplings
    send_pivot_rows(0)
    sum_cores(1)
    send_chips(1)
    late_product(2)
    sum_chips(0, slice(0, 16))
    send_side_rows(0)
    late_product(3)
    send_core(2)
    send_core(3)
    sum_chips(1, slice(16, 32))
    nexts[0].append(send(own[0].at[16:32, :], rest[0].at[0:16, :], partners[0] + (0, 0)))
    for piece in (2, 3):
        sum_cores(piece)
        send_chips(piece)

    eye = jnp.where(
        lax.broadcasted_iota(jnp.int32, (W, W), 0) == lax.broadcasted_iota(jnp.int32, (W, W), 1), 1.0, 0.0
    )
    spread = [[] for _ in range(3)]

    def apply(targets, sources, weights, between):
        w_high, w_low = split(weights.T)
        size = 512
        for c in range(ROWS // size):
            if c == 2:
                between()
            rows = pl.ds(c * size, size)
            wide = [a_buf[i, rows, :] for i in sources]
            high, low = split(wide[0] if len(wide) == 1 else jnp.concatenate(wide, axis=1))
            change = one(high, w_high) + one(low, w_high) + one(high, w_low)
            for k, target in enumerate(targets):
                a_buf[target, rows, :] = a_buf[target, rows, :] - change[:, W * k : W * k + W]

    def blocks(level, b):
        return us[level][:, 16 * b : 16 * b + 16, :].reshape(W, W)

    core_rows = pl.ds(pl.multiple_of(core * 64, 64), 64)
    forward = [[], []]
    coef_forward = [[], []]

    def forward_side_rows(level):
        receive(others[level])
        both = gat[level].at[:, core_rows, W:]
        forward[level].append(send(both, both, (z, x, 0, 1)))

    def forward_coefficients(level):
        receive(spread[level])
        half_of = us[level].at[pl.ds(core * 4, 4)]
        coef_forward[level].append(send(half_of, half_of, (z, x, 0, 1)))

    def send_partner(level, low, top, copies):
        target = rest[level].at[low - 16 : top - 16, :]
        copies[level].append(send(own[level].at[low:top, :], target, partners[level] + (0, 0)))

    def send_coefficients(level):
        for to in near:
            if level < 2 and to[3] == 1:
                continue
            spread[level].append(send(us[level].at[mine], us[level].at[mine], to))

    def advance(level, low, top, copies):
        receive(copies[level])
        gather, inv = gat[level], inv_buf[...]
        p_own, p_sib = gather[0, :, 0:W], gather[1, :, 0:W]
        w_own = own[level][low:top, 0:W]
        w_sib = rest[level][low - 16 : top - 16, 0:W]
        u_own = dot(w_sib - dot(w_own, p_sib), inv)
        u_sib = w_own - dot(u_own, p_own)
        us[level][mine, low - 16 : top - 16, :] = u_own
        own[level + 1][low - 16 : top - 16, :] = (
            own[level][low:top, W:]
            + rest[level][low - 16 : top - 16, W:]
            - dot(u_own, gather[0, :, W:])
            - dot(u_sib, gather[1, :, W:])
        )

    def solve_pivots(level, between=None):
        receive(pivots[level])
        return inverse(eye - dot(gat[level][0, :, 0:W], gat[level][1, :, 0:W]), between)

    mids = [[] for _ in range(4)]

    inv_buf[...] = solve_pivots(0, functools.partial(forward_side_rows, 0))
    receive(forward[0])
    advance(0, 16, 32, nexts)
    send_pivot_rows(1)
    sum_chips(2, slice(32, 48))
    send_partner(0, 32, 48, mids)
    send_side_rows(1)
    sum_chips(3, slice(48, 80))
    send_partner(0, 48, 80, rests)
    advance(0, 32, 48, mids)
    send_partner(1, 16, 32, nexts)

    def late_rows():
        forward_side_rows(1)
        advance(0, 48, 80, rests)
        send_partner(1, 32, 64, rests)
        send_coefficients(0)

    inv = solve_pivots(1, late_rows)
    inv_buf[...] = inv
    receive(forward[1])
    advance(1, 16, 32, nexts)
    send_pivot_rows(2)
    advance(1, 32, 64, rests)

    send_partner(2, 16, 32, nexts)
    send_side_rows(2)
    send_partner(2, 32, 48, rests)
    send_coefficients(1)
    forward_coefficients(0)
    inv_buf[...] = solve_pivots(2)
    receive(others[2])
    forward_coefficients(1)
    advance(2, 16, 32, nexts)
    send_pivot_rows(3)
    advance(2, 32, 48, rests)

    receive(coef_forward[0] + coef_forward[1])
    def last_sends():
        send_side_rows(3)
        send_coefficients(2)

    u3 = jnp.concatenate([blocks(1, b) for b in range(3)], axis=0)
    u4 = jnp.concatenate([blocks(0, b) for b in range(1, 4)], axis=0) - dot(u3, blocks(0, 0))
    apply((2, 3, 4), (0, 1), jnp.concatenate([u4, u3], axis=1), last_sends)
    for copy in started[:-22]:
        copy.wait_send()
    del started[:-22]
    inv = solve_pivots(3)
    receive(others[3])
    y_one = dot(gatx[1] - dot(gatx[0], gat[3][1]), inv)

    receive(spread[2])
    y_two = blocks(2, 1) - dot(y_one, blocks(2, 0))
    w_high, w_low = split(jnp.concatenate([y_two.T, y_one.T], axis=0))
    w_both = jnp.concatenate([w_high, w_low], axis=1)
    stores = []
    size = ROWS // 8
    for c in range(8):
        rows = pl.ds(c * size, size)
        high, low = split(jnp.concatenate([a_buf[2, rows, :], a_buf[3, rows, :]], axis=1))
        both = one(high, w_both)
        a_buf[4, rows, :] = a_buf[4, rows, :] - (both[:, :W] + both[:, W:] + one(low, w_high))
        stores.append(pltpu.make_async_copy(a_buf.at[4, rows, :], out.at[rows, :], out_sems.at[c]))
        stores[-1].start()
    for copy in stores:
        copy.wait()
    for copy in started:
        copy.wait_send()


def body(l4, l3, l2, l1, r4, r3, r2, r1, x):
    f32 = jnp.float32
    hbm = pl.BlockSpec(memory_space=pl.ANY)
    pieces, widths = (16, 16, 16, 32), (384, 512, 512, 512)
    n_copies = 7 + 4 + 12 + 4 * 15 + 2 * 8 + 2 * 15 + 7 + 2 * 4 + 7
    return pl.pallas_call(
        solve_kernel,
        out_shape=jax.ShapeDtypeStruct((ROWS, W), f32),
        in_specs=[hbm] * 9,
        out_specs=hbm,
        scratch_shapes=[
            pltpu.VMEM((5, ROWS, W), f32),
            pltpu.VMEM((4, ROWS, W), f32),
            pltpu.VMEM((ROWS, 512), jnp.bfloat16),
            pltpu.VMEM((ROWS, 512), jnp.bfloat16),
            pltpu.VMEM((384, 512), f32),
            [pltpu.VMEM((2, 4, n, 512), f32) for n in pieces],
            pltpu.VMEM((7, 16, W), f32),
            [pltpu.VMEM((4, n, lanes), f32) for n, lanes in zip(pieces, widths)],
            [pltpu.VMEM((4, n, lanes), f32) for n, lanes in zip(pieces, widths)],
            [pltpu.VMEM((3, n, lanes), f32) for n, lanes in zip(pieces, widths)],
            [pltpu.VMEM((16 * (5 - k), W * (4 - k)), f32) for k in range(4)],
            [pltpu.VMEM((16 * (4 - k), W * (4 - k)), f32) for k in range(3)],
            [pltpu.VMEM((2, W, W * (4 - k)), f32) for k in range(4)],
            pltpu.VMEM((2, W, W), f32),
            [pltpu.VMEM((8, 16 * (4 - k), W), f32) for k in range(3)],
            pltpu.VMEM((W, W), f32),
            pltpu.SemaphoreType.DMA((9, CHUNKS)),
            pltpu.SemaphoreType.DMA((8,)),
            pltpu.SemaphoreType.DMA((2, n_copies)),
        ],
        compiler_params=pltpu.CompilerParams(
            collective_id=0, has_side_effects=True, vmem_limit_bytes=60 * 1024 * 1024
        ),
        name="solve",
    )(l4, l3, l2, l1, x, r4, r3, r2, r1)


def solution(mesh):
    spec = P(("outer", "inner"), None)
    return jax.shard_map(body, mesh=mesh, in_specs=(spec,) * 9, out_specs=spec, check_vma=False)
```

```python
import functools

import jax
import jax.numpy as jnp
from jax import lax
from jax.experimental import pallas as pl
from jax.experimental.pallas import tpu as pltpu
from jax.sharding import PartitionSpec as P

W = 128
HALF = 64
ROWS = 4096
CHUNK = 1024
CHUNKS = ROWS // CHUNK
HIGH = lax.Precision.HIGH
HIGHEST = lax.Precision.HIGHEST
MESH = pl.DeviceIdType.MESH


def dot(a, b, precision=HIGHEST):
    return jnp.dot(a, b, precision=precision, preferred_element_type=jnp.float32)


def split(v):
    high = v.astype(jnp.bfloat16)
    low = (v - high.astype(jnp.float32)).astype(jnp.bfloat16)
    return high, low


def inverse(matrix, between=None):
    lane = lax.broadcasted_iota(jnp.int32, (8, W), 1)
    sub = lax.broadcasted_iota(jnp.int32, (8, W), 0)
    lane_half = lax.broadcasted_iota(jnp.int32, (HALF, W), 1)
    row_whole = lax.broadcasted_iota(jnp.int32, (W, W), 0)

    def column(tile, index):
        return jnp.take_along_axis(tile, jnp.full((8, W), index, jnp.int32), axis=1, mode="promise_in_bounds")

    def spread(tile, i):
        return jnp.broadcast_to(tile[i : i + 1], (8, W))

    def block_step(block, halves):
        start = block * HALF
        panel, rest = halves
        tiles = [panel[8 * i : 8 * i + 8] for i in range(8)]
        for step in range(8):
            begin = start + 8 * step
            inside = (lane >= begin) & (lane < begin + 8)
            cols = [column(tiles[step], begin + i) for i in range(8)]
            pivot = jnp.where(inside, jnp.where(lane == begin + sub, 1.0, 0.0), tiles[step])
            for i in range(0, 8, 2):
                left, right = cols[i], cols[i + 1]
                a, b, c, d = spread(left, i), spread(right, i), spread(left, i + 1), spread(right, i + 1)
                inv = 1.0 / (a * d - b * c)
                at_one, at_two = sub == i, sub == i + 1

                def sweep(tile):
                    one, two = spread(tile, i), spread(tile, i + 1)
                    first = (d * one - b * two) * inv
                    second = (a * two - c * one) * inv
                    other = tile - (left * first + right * second)
                    return jnp.where(at_one, first, jnp.where(at_two, second, other))

                for j in range(i + 2, 8):
                    cols[j] = sweep(cols[j])
                pivot = sweep(pivot)
            rows = [jnp.broadcast_to(pivot[i : i + 1], (8, W)) for i in range(8)]
            for t in range(8):
                if t == step:
                    continue
                terms = [column(tiles[t], begin + i) * rows[i] for i in range(8)]
                while len(terms) > 1:
                    terms = [terms[k] + terms[k + 1] for k in range(0, len(terms), 2)]
                tiles[t] = jnp.where(inside, 0.0, tiles[t]) - terms[0]
            tiles[step] = pivot
        panel = jnp.concatenate(tiles, axis=0)
        tall = jnp.where(
            (row_whole >= start) & (row_whole < start + HALF), jnp.concatenate([panel, panel], axis=0), 0.0
        )
        inside = (lane_half >= start) & (lane_half < start + HALF)
        return jnp.where(inside, 0.0, rest) - dot(rest, tall), panel

    halves = (matrix[:HALF], matrix[HALF:])
    if between is None:
        halves = lax.fori_loop(0, 2, block_step, halves)
    else:
        halves = lax.fori_loop(0, 1, block_step, halves)
        between()
        halves = lax.fori_loop(1, 2, block_step, halves)
    return jnp.concatenate(halves, axis=0)


def solve_kernel(
    l4, l3, l2, l1, x_in, r4, r3, r2, r1, out, a_buf, r_buf, r_high, r_low, acc, h, rx0, rx1, half, rx2,
    own, rest, gat, gatx, us, inv_buf, load_sems, sems,
):
    z = lax.axis_index("outer")
    inner = lax.axis_index("inner")
    x = inner // 8
    y = lax.rem(inner, 8) // 2
    core = lax.rem(inner, 2)
    mine = core * 4 + y

    def device(z_to, x_to, dy, dc):
        y_to = lax.rem(y + dy, 4)
        c_to = lax.rem(core + dc, 2)
        return (z_to, x_to * 8 + y_to * 2 + c_to)

    partners = (
        (z, x + 1 - 2 * lax.rem(x, 2)),
        (z, lax.rem(x + 2, 4)),
        (z + 1 - 2 * lax.rem(z, 2), x),
        (lax.rem(z + 2, 4), x),
    )
    around = [(dy, dc) for dy in (2, 1, 3, 0) for dc in (1, 0)]
    near = [(z, x, dy, dc) for dy, dc in around[:7]]
    far = [[(zp, xp, dy, dc) for dy, dc in around] for zp, xp in partners]
    peers = far[3] + far[1] + far[2] + far[0] + near
    barrier = pltpu.get_barrier_semaphore()
    for peer in peers:
        pl.semaphore_signal(barrier, inc=1, device_id=device(*peer), device_id_type=MESH)

    def load(refs, buffer, offset, k):
        chunks = []
        for c in range(CHUNKS):
            rows = pl.ds(c * CHUNK, CHUNK)
            chunks.append([
                pltpu.make_async_copy(ref.at[rows, :], buffer.at[offset + i, rows, :], load_sems.at[k + i, c])
                for i, ref in enumerate(refs)
            ])
        return chunks

    loads = [r + a for r, a in zip(load((r4, r3, r2, r1), r_buf, 0, 0), load((l4, l3), a_buf, 0, 4))]
    late_loads = load((l2, l1, x_in), a_buf, 2, 6)
    for chunk in loads + late_loads:
        for copy in chunk:
            copy.start()

    count = [0]
    started = []

    def send(src, dst, to):
        k = count[0]
        count[0] += 1
        copy = pltpu.make_async_remote_copy(
            src_ref=src, dst_ref=dst, send_sem=sems.at[0, k], recv_sem=sems.at[1, k],
            device_id=device(*to), device_id_type=MESH,
        )
        copy.start()
        started.append(copy)
        return copy

    def receive(copies):
        for copy in copies:
            copy.wait_recv()

    one = functools.partial(jnp.dot, preferred_element_type=jnp.float32)

    def product(blocks, rows, high, low):
        parts = [split(a_buf[i, rows, :].T) for i in blocks]
        a_high = jnp.concatenate([part[0] for part in parts], axis=0)
        a_low = jnp.concatenate([part[1] for part in parts], axis=0)
        return one(a_high, high) + one(a_low, high) + one(a_high, low)

    total = None
    for c in range(CHUNKS):
        rows = pl.ds(c * CHUNK, CHUNK)
        for copy in loads[c]:
            copy.wait()
        high, low = split(jnp.concatenate([r_buf[i, rows, :] for i in range(4)], axis=1))
        r_high[rows, :] = high
        r_low[rows, :] = low
        total = product((0, 1), rows, high, low)
        if c > 0:
            total = acc[0 : 2 * W, :] + total
        if c < CHUNKS - 1:
            acc[0 : 2 * W, :] = total
    h[0][...] = total[:W].reshape(2, 4, 16, 512)
    h[1][...] = total[W:].reshape(2, 4, 16, 512)
    pl.semaphore_wait(barrier, len(peers))

    def late_product(c):
        rows = pl.ds(c * CHUNK, CHUNK)
        for copy in late_loads[c]:
            copy.wait()
        total = product((2, 3, 4), rows, r_high[rows, :], r_low[rows, :])
        if c > 0:
            total = acc[...] + total
        if c < CHUNKS - 1:
            acc[...] = total
        else:
            h[2][...] = total[:W].reshape(2, 4, 16, 512)
            h[3][:, :, 0:16, :] = total[W : 2 * W].reshape(2, 4, 16, 512)
            h[3][:, :, 16:32, :] = total[2 * W :].reshape(2, 4, 16, 512)

    mine_rows = pl.ds(pl.multiple_of(mine * 16, 16), 16)
    pivots = [[] for _ in range(4)]
    others = [[] for _ in range(4)]
    nexts = [[] for _ in range(4)]
    rests = [[] for _ in range(4)]

    def send_pivot_rows(level):
        mat, gather = own[level], gat[level]
        for side, targets in ((1, far[level]), (0, near)):
            for to in targets:
                pivots[level].append(send(mat.at[0:16, 0:W], gather.at[side, mine_rows, 0:W], to))
        gather[0, mine_rows, 0:W] = mat[0:16, 0:W]

    def send_side_rows(level):
        for side, targets in ((1, far[level]), (0, near)):
            for to in targets:
                if level < 2 and to[3] == 1:
                    continue
                if level < 3:
                    copy = send(own[level].at[0:16, W:], gat[level].at[side, mine_rows, W:], to)
                else:
                    copy = send(own[3].at[16:32, :], gatx.at[side, mine_rows, :], to)
                others[level].append(copy)
        if level == 3:
            gatx[0, mine_rows, :] = own[3][16:32, :]
        else:
            gat[level][0, mine_rows, W:] = own[level][0:16, W:]

    first = [None] * 4
    second = [None] * 4

    def send_core(piece):
        low = W if piece == 0 else 0
        first[piece] = send(h[piece].at[1 - core, :, :, low:], rx1[piece], (z, x, 0, 1))

    def sum_cores(piece):
        receive([first[piece]])
        low = W if piece == 0 else 0
        half[piece][...] = h[piece][core, :, :, low:] + rx1[piece][...]

    def send_chips(piece):
        second[piece] = [
            send(half[piece].at[lax.rem(y + dy, 4)], rx2[piece].at[dy - 1], (z, x, dy, 0)) for dy in (2, 1, 3)
        ]

    def sum_chips(piece, rows):
        receive(second[piece])
        low = W if piece == 0 else 0
        own[0][rows, low:] = half[piece][y] + rx2[piece][0] + rx2[piece][1] + rx2[piece][2]

    direct = []
    for k, (_, _, dy, dc) in enumerate(near):
        piece = h[0].at[lax.rem(core + dc, 2), lax.rem(y + dy, 4), :, 0:W]
        direct.append(send(piece, rx0.at[k], (z, x, dy, dc)))
    send_core(0)
    send_core(1)
    late_product(0)
    for piece in (0, 1):
        sum_cores(piece)
        send_chips(piece)
    late_product(1)
    receive(direct)
    couplings = h[0][core, y, :, 0:W]
    for k in range(7):
        couplings = couplings + rx0[k]
    own[0][0:16, 0:W] = couplings
    send_pivot_rows(0)
    late_product(2)
    sum_chips(0, slice(0, 16))
    send_side_rows(0)
    late_product(3)
    send_core(2)
    send_core(3)
    sum_chips(1, slice(16, 32))
    nexts[0].append(send(own[0].at[16:32, :], rest[0].at[0:16, :], partners[0] + (0, 0)))
    for piece in (2, 3):
        sum_cores(piece)
        send_chips(piece)

    eye = jnp.where(
        lax.broadcasted_iota(jnp.int32, (W, W), 0) == lax.broadcasted_iota(jnp.int32, (W, W), 1), 1.0, 0.0
    )
    spread = [[] for _ in range(3)]

    def apply(targets, sources, weights, between):
        w_high, w_low = split(weights.T)
        size = 512
        for c in range(ROWS // size):
            if c == 5:
                between()
            rows = pl.ds(c * size, size)
            wide = [a_buf[i, rows, :] for i in sources]
            high, low = split(wide[0] if len(wide) == 1 else jnp.concatenate(wide, axis=1))
            change = one(high, w_high) + one(low, w_high) + one(high, w_low)
            for k, target in enumerate(targets):
                a_buf[target, rows, :] = a_buf[target, rows, :] - change[:, W * k : W * k + W]

    def blocks(level, b):
        return us[level][:, 16 * b : 16 * b + 16, :].reshape(W, W)

    core_rows = pl.ds(pl.multiple_of(core * 64, 64), 64)
    forward = [[], []]
    coef_forward = [[], []]

    def forward_side_rows(level):
        receive(others[level])
        both = gat[level].at[:, core_rows, W:]
        forward[level].append(send(both, both, (z, x, 0, 1)))

    def forward_coefficients(level):
        receive(spread[level])
        half_of = us[level].at[pl.ds(core * 4, 4)]
        coef_forward[level].append(send(half_of, half_of, (z, x, 0, 1)))

    def send_partner(level, low, top, copies):
        target = rest[level].at[low - 16 : top - 16, :]
        copies[level].append(send(own[level].at[low:top, :], target, partners[level] + (0, 0)))

    def send_coefficients(level):
        for to in near:
            if level < 2 and to[3] == 1:
                continue
            spread[level].append(send(us[level].at[mine], us[level].at[mine], to))

    def advance(level, low, top, copies):
        receive(copies[level])
        gather, inv = gat[level], inv_buf[...]
        p_own, p_sib = gather[0, :, 0:W], gather[1, :, 0:W]
        w_own = own[level][low:top, 0:W]
        w_sib = rest[level][low - 16 : top - 16, 0:W]
        u_own = dot(w_sib - dot(w_own, p_sib, HIGH), inv, HIGH)
        u_sib = w_own - dot(u_own, p_own, HIGH)
        us[level][mine, low - 16 : top - 16, :] = u_own
        own[level + 1][low - 16 : top - 16, :] = (
            own[level][low:top, W:]
            + rest[level][low - 16 : top - 16, W:]
            - dot(u_own, gather[0, :, W:], HIGH)
            - dot(u_sib, gather[1, :, W:], HIGH)
        )

    def solve_pivots(level, between=None):
        receive(pivots[level])
        return inverse(eye - dot(gat[level][0, :, 0:W], gat[level][1, :, 0:W]), between)

    mids = [[] for _ in range(4)]

    inv_buf[...] = solve_pivots(0, functools.partial(forward_side_rows, 0))
    receive(forward[0])
    advance(0, 16, 32, nexts)
    send_pivot_rows(1)
    sum_chips(2, slice(32, 48))
    send_partner(0, 32, 48, mids)
    send_side_rows(1)
    sum_chips(3, slice(48, 80))
    send_partner(0, 48, 80, rests)
    advance(0, 32, 48, mids)
    send_partner(1, 16, 32, nexts)

    def late_rows():
        forward_side_rows(1)
        advance(0, 48, 80, rests)
        send_partner(1, 32, 64, rests)
        send_coefficients(0)

    inv = solve_pivots(1, late_rows)
    inv_buf[...] = inv
    receive(forward[1])
    advance(1, 16, 32, nexts)
    send_pivot_rows(2)
    advance(1, 32, 64, rests)

    send_partner(2, 16, 32, nexts)
    send_side_rows(2)
    send_partner(2, 32, 48, rests)
    send_coefficients(1)
    forward_coefficients(0)
    inv_buf[...] = solve_pivots(2)
    receive(others[2])
    forward_coefficients(1)
    advance(2, 16, 32, nexts)
    send_pivot_rows(3)
    advance(2, 32, 48, rests)

    receive(coef_forward[0] + coef_forward[1])
    def last_sends():
        send_side_rows(3)
        send_coefficients(2)

    u3 = jnp.concatenate([blocks(1, b) for b in range(3)], axis=0)
    u4 = jnp.concatenate([blocks(0, b) for b in range(1, 4)], axis=0) - dot(u3, blocks(0, 0))
    apply((2, 3, 4), (0, 1), jnp.concatenate([u4, u3], axis=1), last_sends)
    for copy in started[:-22]:
        copy.wait_send()
    del started[:-22]
    inv = solve_pivots(3)
    receive(others[3])
    y_one = dot(gatx[1] - dot(gatx[0], gat[3][1]), inv)

    receive(spread[2])
    y_two = blocks(2, 1) - dot(y_one, blocks(2, 0))
    w_high, w_low = split(jnp.concatenate([y_two.T, y_one.T], axis=0))
    w_both = jnp.concatenate([w_high, w_low], axis=1)
    size = ROWS // 8
    for c in range(8):
        rows = pl.ds(c * size, size)
        high, low = split(jnp.concatenate([a_buf[2, rows, :], a_buf[3, rows, :]], axis=1))
        both = one(high, w_both)
        out[rows, :] = a_buf[4, rows, :] - (both[:, :W] + both[:, W:] + one(low, w_high))
    for copy in started:
        copy.wait_send()


def body(l4, l3, l2, l1, r4, r3, r2, r1, x):
    f32 = jnp.float32
    hbm = pl.BlockSpec(memory_space=pl.ANY)
    pieces, widths = (16, 16, 16, 32), (384, 512, 512, 512)
    n_copies = 7 + 4 + 12 + 4 * 15 + 2 * 8 + 2 * 15 + 7 + 2 * 4 + 7
    return pl.pallas_call(
        solve_kernel,
        out_shape=jax.ShapeDtypeStruct((ROWS, W), f32),
        in_specs=[hbm] * 9,
        out_specs=pl.BlockSpec(memory_space=pltpu.VMEM),
        scratch_shapes=[
            pltpu.VMEM((5, ROWS, W), f32),
            pltpu.VMEM((4, ROWS, W), f32),
            pltpu.VMEM((ROWS, 512), jnp.bfloat16),
            pltpu.VMEM((ROWS, 512), jnp.bfloat16),
            pltpu.VMEM((384, 512), f32),
            [pltpu.VMEM((2, 4, n, 512), f32) for n in pieces],
            pltpu.VMEM((7, 16, W), f32),
            [pltpu.VMEM((4, n, lanes), f32) for n, lanes in zip(pieces, widths)],
            [pltpu.VMEM((4, n, lanes), f32) for n, lanes in zip(pieces, widths)],
            [pltpu.VMEM((3, n, lanes), f32) for n, lanes in zip(pieces, widths)],
            [pltpu.VMEM((16 * (5 - k), W * (4 - k)), f32) for k in range(4)],
            [pltpu.VMEM((16 * (4 - k), W * (4 - k)), f32) for k in range(3)],
            [pltpu.VMEM((2, W, W * (4 - k)), f32) for k in range(4)],
            pltpu.VMEM((2, W, W), f32),
            [pltpu.VMEM((8, 16 * (4 - k), W), f32) for k in range(3)],
            pltpu.VMEM((W, W), f32),
            pltpu.SemaphoreType.DMA((9, CHUNKS)),
            pltpu.SemaphoreType.DMA((2, n_copies)),
        ],
        compiler_params=pltpu.CompilerParams(
            collective_id=0, has_side_effects=True, vmem_limit_bytes=50 * 1024 * 1024
        ),
        name="solve",
    )(l4, l3, l2, l1, x, r4, r3, r2, r1)


def solution(mesh):
    spec = P(("outer", "inner"), None)
    return jax.shard_map(body, mesh=mesh, in_specs=(spec,) * 9, out_specs=spec, check_vma=False)
```

```python
import functools

import jax
import jax.numpy as jnp
from jax import lax
from jax.experimental import pallas as pl
from jax.experimental.pallas import tpu as pltpu
from jax.sharding import PartitionSpec as P

W = 128
HALF = 64
ROWS = 4096
CHUNK = 1024
CHUNKS = ROWS // CHUNK
HIGH = lax.Precision.HIGH
HIGHEST = lax.Precision.HIGHEST
MESH = pl.DeviceIdType.MESH


def dot(a, b, precision=HIGHEST):
    return jnp.dot(a, b, precision=precision, preferred_element_type=jnp.float32)


def split(v):
    high = v.astype(jnp.bfloat16)
    low = (v - high.astype(jnp.float32)).astype(jnp.bfloat16)
    return high, low


def inverse(matrix, between=None):
    lane = lax.broadcasted_iota(jnp.int32, (8, W), 1)
    sub = lax.broadcasted_iota(jnp.int32, (8, W), 0)
    lane_half = lax.broadcasted_iota(jnp.int32, (HALF, W), 1)
    row_whole = lax.broadcasted_iota(jnp.int32, (W, W), 0)

    def column(tile, index):
        return jnp.take_along_axis(tile, jnp.full((8, W), index, jnp.int32), axis=1, mode="promise_in_bounds")

    def spread(tile, i):
        return jnp.broadcast_to(tile[i : i + 1], (8, W))

    def block_step(block, halves):
        start = block * HALF
        panel, rest = halves
        tiles = [panel[8 * i : 8 * i + 8] for i in range(8)]
        for step in range(8):
            begin = start + 8 * step
            inside = (lane >= begin) & (lane < begin + 8)
            cols = [column(tiles[step], begin + i) for i in range(8)]
            pivot = jnp.where(inside, jnp.where(lane == begin + sub, 1.0, 0.0), tiles[step])
            for i in range(0, 8, 2):
                left, right = cols[i], cols[i + 1]
                a, b, c, d = spread(left, i), spread(right, i), spread(left, i + 1), spread(right, i + 1)
                inv = 1.0 / (a * d - b * c)
                at_one, at_two = sub == i, sub == i + 1

                def sweep(tile):
                    one, two = spread(tile, i), spread(tile, i + 1)
                    first = (d * one - b * two) * inv
                    second = (a * two - c * one) * inv
                    other = tile - (left * first + right * second)
                    return jnp.where(at_one, first, jnp.where(at_two, second, other))

                for j in range(i + 2, 8):
                    cols[j] = sweep(cols[j])
                pivot = sweep(pivot)
            rows = [jnp.broadcast_to(pivot[i : i + 1], (8, W)) for i in range(8)]
            for t in range(8):
                if t == step:
                    continue
                terms = [column(tiles[t], begin + i) * rows[i] for i in range(8)]
                while len(terms) > 1:
                    terms = [terms[k] + terms[k + 1] for k in range(0, len(terms), 2)]
                tiles[t] = jnp.where(inside, 0.0, tiles[t]) - terms[0]
            tiles[step] = pivot
        panel = jnp.concatenate(tiles, axis=0)
        tall = jnp.where(
            (row_whole >= start) & (row_whole < start + HALF), jnp.concatenate([panel, panel], axis=0), 0.0
        )
        inside = (lane_half >= start) & (lane_half < start + HALF)
        return jnp.where(inside, 0.0, rest) - dot(rest, tall), panel

    halves = (matrix[:HALF], matrix[HALF:])
    halves = block_step(0, halves)
    if between is not None:
        between()
    halves = block_step(1, halves)
    return jnp.concatenate(halves, axis=0)


def solve_kernel(
    l4, l3, l2, l1, x_in, r4, r3, r2, r1, out, a_buf, r_buf, r_high, r_low, acc, h, rx0, rx1, half, rx2,
    own, rest, gat, gatx, us, inv_buf, load_sems, sems,
):
    z = lax.axis_index("outer")
    inner = lax.axis_index("inner")
    x = inner // 8
    y = lax.rem(inner, 8) // 2
    core = lax.rem(inner, 2)
    mine = core * 4 + y

    def device(z_to, x_to, dy, dc):
        y_to = lax.rem(y + dy, 4)
        c_to = lax.rem(core + dc, 2)
        return (z_to, x_to * 8 + y_to * 2 + c_to)

    partners = (
        (z, x + 1 - 2 * lax.rem(x, 2)),
        (z, lax.rem(x + 2, 4)),
        (z + 1 - 2 * lax.rem(z, 2), x),
        (lax.rem(z + 2, 4), x),
    )
    around = [(dy, dc) for dy in (2, 1, 3, 0) for dc in (1, 0)]
    near = [(z, x, dy, dc) for dy, dc in around[:7]]
    far = [[(zp, xp, dy, dc) for dy, dc in around] for zp, xp in partners]
    peers = far[3] + far[1] + far[2] + far[0] + near
    barrier = pltpu.get_barrier_semaphore()
    for peer in peers:
        pl.semaphore_signal(barrier, inc=1, device_id=device(*peer), device_id_type=MESH)

    def load(refs, buffer, offset, k):
        chunks = []
        for c in range(CHUNKS):
            rows = pl.ds(c * CHUNK, CHUNK)
            chunks.append([
                pltpu.make_async_copy(ref.at[rows, :], buffer.at[offset + i, rows, :], load_sems.at[k + i, c])
                for i, ref in enumerate(refs)
            ])
        return chunks

    loads = [r + a for r, a in zip(load((r4, r3, r2, r1), r_buf, 0, 0), load((l4, l3), a_buf, 0, 4))]
    late_loads = load((l2, l1, x_in), a_buf, 2, 6)
    for chunk in loads + late_loads:
        for copy in chunk:
            copy.start()

    count = [0]
    started = []

    def send(src, dst, to):
        k = count[0]
        count[0] += 1
        copy = pltpu.make_async_remote_copy(
            src_ref=src, dst_ref=dst, send_sem=sems.at[0, k], recv_sem=sems.at[1, k],
            device_id=device(*to), device_id_type=MESH,
        )
        copy.start()
        started.append(copy)
        return copy

    def receive(copies):
        for copy in copies:
            copy.wait_recv()

    one = functools.partial(jnp.dot, preferred_element_type=jnp.float32)

    def product(blocks, rows, high, low):
        parts = [split(a_buf[i, rows, :].T) for i in blocks]
        a_high = jnp.concatenate([part[0] for part in parts], axis=0)
        a_low = jnp.concatenate([part[1] for part in parts], axis=0)
        return one(a_high, high) + one(a_low, high) + one(a_high, low)

    total = None
    for c in range(CHUNKS):
        rows = pl.ds(c * CHUNK, CHUNK)
        for copy in loads[c]:
            copy.wait()
        high, low = split(jnp.concatenate([r_buf[i, rows, :] for i in range(4)], axis=1))
        r_high[rows, :] = high
        r_low[rows, :] = low
        total = product((0, 1), rows, high, low)
        if c > 0:
            total = acc[0 : 2 * W, :] + total
        if c < CHUNKS - 1:
            acc[0 : 2 * W, :] = total
    h[0][...] = total[:W].reshape(2, 4, 16, 512)
    h[1][...] = total[W:].reshape(2, 4, 16, 512)
    pl.semaphore_wait(barrier, len(peers))

    def late_product(c):
        rows = pl.ds(c * CHUNK, CHUNK)
        for copy in late_loads[c]:
            copy.wait()
        total = product((2, 3, 4), rows, r_high[rows, :], r_low[rows, :])
        if c > 0:
            total = acc[...] + total
        if c < CHUNKS - 1:
            acc[...] = total
        else:
            h[2][...] = total[:W].reshape(2, 4, 16, 512)
            h[3][:, :, 0:16, :] = total[W : 2 * W].reshape(2, 4, 16, 512)
            h[3][:, :, 16:32, :] = total[2 * W :].reshape(2, 4, 16, 512)

    mine_rows = pl.ds(pl.multiple_of(mine * 16, 16), 16)
    pivots = [[] for _ in range(4)]
    others = [[] for _ in range(4)]
    nexts = [[] for _ in range(4)]
    rests = [[] for _ in range(4)]

    def send_pivot_rows(level):
        mat, gather = own[level], gat[level]
        for side, targets in ((1, far[level]), (0, near)):
            for to in targets:
                pivots[level].append(send(mat.at[0:16, 0:W], gather.at[side, mine_rows, 0:W], to))
        gather[0, mine_rows, 0:W] = mat[0:16, 0:W]

    def send_side_rows(level):
        for side, targets in ((1, far[level]), (0, near)):
            for to in targets:
                if level < 2 and to[3] == 1:
                    continue
                if level < 3:
                    copy = send(own[level].at[0:16, W:], gat[level].at[side, mine_rows, W:], to)
                else:
                    copy = send(own[3].at[16:32, :], gatx.at[side, mine_rows, :], to)
                others[level].append(copy)
        if level == 3:
            gatx[0, mine_rows, :] = own[3][16:32, :]
        else:
            gat[level][0, mine_rows, W:] = own[level][0:16, W:]

    first = [None] * 4
    second = [None] * 4

    def send_core(piece):
        low = W if piece == 0 else 0
        first[piece] = send(h[piece].at[1 - core, :, :, low:], rx1[piece], (z, x, 0, 1))

    def sum_cores(piece):
        receive([first[piece]])
        low = W if piece == 0 else 0
        half[piece][...] = h[piece][core, :, :, low:] + rx1[piece][...]

    def send_chips(piece):
        second[piece] = [
            send(half[piece].at[lax.rem(y + dy, 4)], rx2[piece].at[dy - 1], (z, x, dy, 0)) for dy in (2, 1, 3)
        ]

    def sum_chips(piece, rows):
        receive(second[piece])
        low = W if piece == 0 else 0
        own[0][rows, low:] = half[piece][y] + rx2[piece][0] + rx2[piece][1] + rx2[piece][2]

    direct = []
    for k, (_, _, dy, dc) in enumerate(near):
        piece = h[0].at[lax.rem(core + dc, 2), lax.rem(y + dy, 4), :, 0:W]
        direct.append(send(piece, rx0.at[k], (z, x, dy, dc)))
    send_core(0)
    send_core(1)
    late_product(0)
    for piece in (0, 1):
        sum_cores(piece)
        send_chips(piece)
    late_product(1)
    receive(direct)
    couplings = h[0][core, y, :, 0:W]
    for k in range(7):
        couplings = couplings + rx0[k]
    own[0][0:16, 0:W] = couplings
    send_pivot_rows(0)
    late_product(2)
    sum_chips(0, slice(0, 16))
    send_side_rows(0)
    late_product(3)
    send_core(2)
    send_core(3)
    sum_chips(1, slice(16, 32))
    nexts[0].append(send(own[0].at[16:32, :], rest[0].at[0:16, :], partners[0] + (0, 0)))
    for piece in (2, 3):
        sum_cores(piece)
        send_chips(piece)

    eye = jnp.where(
        lax.broadcasted_iota(jnp.int32, (W, W), 0) == lax.broadcasted_iota(jnp.int32, (W, W), 1), 1.0, 0.0
    )
    spread = [[] for _ in range(3)]

    def apply(targets, sources, weights, between):
        w_high, w_low = split(weights.T)
        size = 512
        for c in range(ROWS // size):
            if c == 2:
                between()
            rows = pl.ds(c * size, size)
            wide = [a_buf[i, rows, :] for i in sources]
            high, low = split(wide[0] if len(wide) == 1 else jnp.concatenate(wide, axis=1))
            change = one(high, w_high) + one(low, w_high) + one(high, w_low)
            for k, target in enumerate(targets):
                a_buf[target, rows, :] = a_buf[target, rows, :] - change[:, W * k : W * k + W]

    def blocks(level, b):
        return us[level][:, 16 * b : 16 * b + 16, :].reshape(W, W)

    core_rows = pl.ds(pl.multiple_of(core * 64, 64), 64)
    forward = [[], []]
    forward_late = [[], []]
    coef_forward = [[], []]

    def forward_side_rows(level):
        receive(others[level])
        both = gat[level].at[:, core_rows, W : 2 * W]
        forward[level].append(send(both, both, (z, x, 0, 1)))
        both = gat[level].at[:, core_rows, 2 * W :]
        forward_late[level].append(send(both, both, (z, x, 0, 1)))

    def forward_coefficients(level):
        receive(spread[level])
        half_of = us[level].at[pl.ds(core * 4, 4)]
        coef_forward[level].append(send(half_of, half_of, (z, x, 0, 1)))

    def send_partner(level, low, top, copies):
        target = rest[level].at[low - 16 : top - 16, :]
        copies[level].append(send(own[level].at[low:top, :], target, partners[level] + (0, 0)))

    def send_coefficients(level):
        for to in near:
            if level < 2 and to[3] == 1:
                continue
            spread[level].append(send(us[level].at[mine], us[level].at[mine], to))

    def advance(level, low, top, copies):
        receive(copies[level])
        gather, inv = gat[level], inv_buf[...]
        p_own, p_sib = gather[0, :, 0:W], gather[1, :, 0:W]
        w_own = own[level][low:top, 0:W]
        w_sib = rest[level][low - 16 : top - 16, 0:W]
        u_own = dot(w_sib - dot(w_own, p_sib, HIGH), inv, HIGH)
        u_sib = w_own - dot(u_own, p_own, HIGH)
        us[level][mine, low - 16 : top - 16, :] = u_own
        own[level + 1][low - 16 : top - 16, :] = (
            own[level][low:top, W:]
            + rest[level][low - 16 : top - 16, W:]
            - dot(u_own, gather[0, :, W:], HIGH)
            - dot(u_sib, gather[1, :, W:], HIGH)
        )

    def advance_pivots(level):
        receive(nexts[level])
        gather, inv = gat[level], inv_buf[...]
        p_own, p_sib = gather[0, :, 0:W], gather[1, :, 0:W]
        w_own = own[level][16:32, 0:W]
        u_own = dot(rest[level][0:16, 0:W] - dot(w_own, p_sib, HIGH), inv, HIGH)
        u_sib = w_own - dot(u_own, p_own, HIGH)
        us[level][mine, 0:16, :] = u_own

        def pass_on(low, top):
            own[level + 1][0:16, low - W : top - W] = (
                own[level][16:32, low:top]
                + rest[level][0:16, low:top]
                - dot(u_own, gather[0, :, low:top], HIGH)
                - dot(u_sib, gather[1, :, low:top], HIGH)
            )

        pass_on(W, 2 * W)
        send_pivot_rows(level + 1)
        if level < 2:
            receive(forward_late[level])
            pass_on(2 * W, (4 - level) * W)

    def solve_pivots(level, between=None):
        receive(pivots[level])
        return inverse(eye - dot(gat[level][0, :, 0:W], gat[level][1, :, 0:W]), between)

    mids = [[] for _ in range(4)]

    inv_buf[...] = solve_pivots(0, functools.partial(forward_side_rows, 0))
    receive(forward[0])
    advance_pivots(0)
    sum_chips(2, slice(32, 48))
    send_partner(0, 32, 48, mids)
    send_side_rows(1)
    sum_chips(3, slice(48, 80))
    send_partner(0, 48, 80, rests)
    advance(0, 32, 48, mids)
    send_partner(1, 16, 32, nexts)

    def late_rows():
        forward_side_rows(1)
        advance(0, 48, 80, rests)
        send_partner(1, 32, 64, rests)

    inv = solve_pivots(1, late_rows)
    inv_buf[...] = inv
    receive(forward[1])
    advance_pivots(1)
    advance(1, 32, 64, rests)

    send_side_rows(2)
    send_partner(2, 16, 32, nexts)
    send_partner(2, 32, 48, rests)
    send_coefficients(0)
    send_coefficients(1)
    inv_buf[...] = solve_pivots(2)
    receive(others[2])
    forward_coefficients(0)
    forward_coefficients(1)
    advance_pivots(2)
    advance(2, 32, 48, rests)

    receive(coef_forward[0] + coef_forward[1])
    def last_sends():
        send_side_rows(3)
        send_coefficients(2)

    u3 = jnp.concatenate([blocks(1, b) for b in range(3)], axis=0)
    u4 = jnp.concatenate([blocks(0, b) for b in range(1, 4)], axis=0) - dot(u3, blocks(0, 0))
    apply((2, 3, 4), (0, 1), jnp.concatenate([u4, u3], axis=1), last_sends)
    for copy in started[:-22]:
        copy.wait_send()
    del started[:-22]
    inv = solve_pivots(3)
    receive(others[3])
    y_one = dot(gatx[1] - dot(gatx[0], gat[3][1]), inv)

    receive(spread[2])
    y_two = blocks(2, 1) - dot(y_one, blocks(2, 0))
    w_high, w_low = split(jnp.concatenate([y_two.T, y_one.T], axis=0))
    w_both = jnp.concatenate([w_high, w_low], axis=1)
    size = ROWS // 8
    for c in range(8):
        rows = pl.ds(c * size, size)
        high, low = split(jnp.concatenate([a_buf[2, rows, :], a_buf[3, rows, :]], axis=1))
        both = one(high, w_both)
        out[rows, :] = a_buf[4, rows, :] - (both[:, :W] + both[:, W:] + one(low, w_high))
    for copy in started:
        copy.wait_send()


def body(l4, l3, l2, l1, r4, r3, r2, r1, x):
    f32 = jnp.float32
    hbm = pl.BlockSpec(memory_space=pl.ANY)
    pieces, widths = (16, 16, 16, 32), (384, 512, 512, 512)
    n_copies = 7 + 4 + 12 + 4 * 15 + 2 * 9 + 2 * 15 + 7 + 2 * 4 + 7
    return pl.pallas_call(
        solve_kernel,
        out_shape=jax.ShapeDtypeStruct((ROWS, W), f32),
        in_specs=[hbm] * 9,
        out_specs=pl.BlockSpec(memory_space=pltpu.VMEM),
        scratch_shapes=[
            pltpu.VMEM((5, ROWS, W), f32),
            pltpu.VMEM((4, ROWS, W), f32),
            pltpu.VMEM((ROWS, 512), jnp.bfloat16),
            pltpu.VMEM((ROWS, 512), jnp.bfloat16),
            pltpu.VMEM((384, 512), f32),
            [pltpu.VMEM((2, 4, n, 512), f32) for n in pieces],
            pltpu.VMEM((7, 16, W), f32),
            [pltpu.VMEM((4, n, lanes), f32) for n, lanes in zip(pieces, widths)],
            [pltpu.VMEM((4, n, lanes), f32) for n, lanes in zip(pieces, widths)],
            [pltpu.VMEM((3, n, lanes), f32) for n, lanes in zip(pieces, widths)],
            [pltpu.VMEM((16 * (5 - k), W * (4 - k)), f32) for k in range(4)],
            [pltpu.VMEM((16 * (4 - k), W * (4 - k)), f32) for k in range(3)],
            [pltpu.VMEM((2, W, W * (4 - k)), f32) for k in range(4)],
            pltpu.VMEM((2, W, W), f32),
            [pltpu.VMEM((8, 16 * (4 - k), W), f32) for k in range(3)],
            pltpu.VMEM((W, W), f32),
            pltpu.SemaphoreType.DMA((9, CHUNKS)),
            pltpu.SemaphoreType.DMA((2, n_copies)),
        ],
        compiler_params=pltpu.CompilerParams(
            collective_id=0, has_side_effects=True, vmem_limit_bytes=50 * 1024 * 1024
        ),
        name="solve",
    )(l4, l3, l2, l1, x, r4, r3, r2, r1)


def solution(mesh):
    spec = P(("outer", "inner"), None)
    return jax.shard_map(body, mesh=mesh, in_specs=(spec,) * 9, out_specs=spec, check_vma=False)
```

```python
import functools

import jax
import jax.numpy as jnp
from jax import lax
from jax.experimental import pallas as pl
from jax.experimental.pallas import tpu as pltpu
from jax.sharding import PartitionSpec as P

W = 128
HALF = 64
ROWS = 4096
CHUNK = 1024
CHUNKS = ROWS // CHUNK
HIGH = lax.Precision.HIGH
HIGHEST = lax.Precision.HIGHEST
MESH = pl.DeviceIdType.MESH


def dot(a, b, precision=HIGHEST):
    return jnp.dot(a, b, precision=precision, preferred_element_type=jnp.float32)


def split(v):
    high = v.astype(jnp.bfloat16)
    low = (v - high.astype(jnp.float32)).astype(jnp.bfloat16)
    return high, low


def inverse(matrix, between=None):
    lane = lax.broadcasted_iota(jnp.int32, (8, W), 1)
    sub = lax.broadcasted_iota(jnp.int32, (8, W), 0)
    lane_half = lax.broadcasted_iota(jnp.int32, (HALF, W), 1)
    row_whole = lax.broadcasted_iota(jnp.int32, (W, W), 0)

    def column(tile, index):
        return jnp.take_along_axis(tile, jnp.full((8, W), index, jnp.int32), axis=1, mode="promise_in_bounds")

    def spread(tile, i):
        return jnp.broadcast_to(tile[i : i + 1], (8, W))

    def block_step(block, halves):
        start = block * HALF
        panel, rest = halves
        tiles = [panel[8 * i : 8 * i + 8] for i in range(8)]
        for step in range(8):
            begin = start + 8 * step
            inside = (lane >= begin) & (lane < begin + 8)
            cols = [column(tiles[step], begin + i) for i in range(8)]
            pivot = jnp.where(inside, jnp.where(lane == begin + sub, 1.0, 0.0), tiles[step])
            for i in range(0, 8, 2):
                left, right = cols[i], cols[i + 1]
                a, b, c, d = spread(left, i), spread(right, i), spread(left, i + 1), spread(right, i + 1)
                inv = 1.0 / (a * d - b * c)
                at_one, at_two = sub == i, sub == i + 1

                def sweep(tile):
                    one, two = spread(tile, i), spread(tile, i + 1)
                    first = (d * one - b * two) * inv
                    second = (a * two - c * one) * inv
                    other = tile - (left * first + right * second)
                    return jnp.where(at_one, first, jnp.where(at_two, second, other))

                for j in range(i + 2, 8):
                    cols[j] = sweep(cols[j])
                pivot = sweep(pivot)
            rows = [jnp.broadcast_to(pivot[i : i + 1], (8, W)) for i in range(8)]
            for t in range(8):
                if t == step:
                    continue
                terms = [column(tiles[t], begin + i) * rows[i] for i in range(8)]
                while len(terms) > 1:
                    terms = [terms[k] + terms[k + 1] for k in range(0, len(terms), 2)]
                tiles[t] = jnp.where(inside, 0.0, tiles[t]) - terms[0]
            tiles[step] = pivot
        panel = jnp.concatenate(tiles, axis=0)
        tall = jnp.where(
            (row_whole >= start) & (row_whole < start + HALF), jnp.concatenate([panel, panel], axis=0), 0.0
        )
        inside = (lane_half >= start) & (lane_half < start + HALF)
        return jnp.where(inside, 0.0, rest) - dot(rest, tall), panel

    halves = (matrix[:HALF], matrix[HALF:])
    halves = block_step(0, halves)
    if between is not None:
        between()
    halves = block_step(1, halves)
    return jnp.concatenate(halves, axis=0)


def solve_kernel(
    l4, l3, l2, l1, x_in, r4, r3, r2, r1, out, a_buf, r_buf, r_high, r_low, acc, h, rx0, rx1, half, rx2,
    own, rest, gat, gatx, us, inv_buf, load_sems, sems,
):
    z = lax.axis_index("outer")
    inner = lax.axis_index("inner")
    x = inner // 8
    y = lax.rem(inner, 8) // 2
    core = lax.rem(inner, 2)
    mine = core * 4 + y

    def device(z_to, x_to, dy, dc):
        y_to = lax.rem(y + dy, 4)
        c_to = lax.rem(core + dc, 2)
        return (z_to, x_to * 8 + y_to * 2 + c_to)

    partners = (
        (z, x + 1 - 2 * lax.rem(x, 2)),
        (z, lax.rem(x + 2, 4)),
        (z + 1 - 2 * lax.rem(z, 2), x),
        (lax.rem(z + 2, 4), x),
    )
    around = [(dy, dc) for dy in (2, 1, 3, 0) for dc in (1, 0)]
    near = [(z, x, dy, dc) for dy, dc in around[:7]]
    far = [[(zp, xp, dy, dc) for dy, dc in around] for zp, xp in partners]
    peers = far[3] + far[1] + far[2] + far[0] + near
    barrier = pltpu.get_barrier_semaphore()
    for peer in peers:
        pl.semaphore_signal(barrier, inc=1, device_id=device(*peer), device_id_type=MESH)

    def load(refs, buffer, offset, k):
        chunks = []
        for c in range(CHUNKS):
            rows = pl.ds(c * CHUNK, CHUNK)
            chunks.append([
                pltpu.make_async_copy(ref.at[rows, :], buffer.at[offset + i, rows, :], load_sems.at[k + i, c])
                for i, ref in enumerate(refs)
            ])
        return chunks

    loads = [r + a for r, a in zip(load((r4, r3, r2, r1), r_buf, 0, 0), load((l4, l3), a_buf, 0, 4))]
    late_loads = load((l2, l1, x_in), a_buf, 2, 6)
    for chunk in loads + late_loads:
        for copy in chunk:
            copy.start()

    count = [0]
    started = []

    def send(src, dst, to):
        k = count[0]
        count[0] += 1
        copy = pltpu.make_async_remote_copy(
            src_ref=src, dst_ref=dst, send_sem=sems.at[0, k], recv_sem=sems.at[1, k],
            device_id=device(*to), device_id_type=MESH,
        )
        copy.start()
        started.append(copy)
        return copy

    def receive(copies):
        for copy in copies:
            copy.wait_recv()

    one = functools.partial(jnp.dot, preferred_element_type=jnp.float32)

    def product(blocks, rows, high, low):
        parts = [split(a_buf[i, rows, :].T) for i in blocks]
        a_high = jnp.concatenate([part[0] for part in parts], axis=0)
        a_low = jnp.concatenate([part[1] for part in parts], axis=0)
        return one(a_high, high) + one(a_low, high) + one(a_high, low)

    total = None
    for c in range(CHUNKS):
        rows = pl.ds(c * CHUNK, CHUNK)
        for copy in loads[c]:
            copy.wait()
        high, low = split(jnp.concatenate([r_buf[i, rows, :] for i in range(4)], axis=1))
        r_high[rows, :] = high
        r_low[rows, :] = low
        total = product((0, 1), rows, high, low)
        if c > 0:
            total = acc[0 : 2 * W, :] + total
        if c < CHUNKS - 1:
            acc[0 : 2 * W, :] = total
    h[0][...] = total[:W].reshape(2, 4, 16, 512)
    h[1][...] = total[W:].reshape(2, 4, 16, 512)
    pl.semaphore_wait(barrier, len(peers))

    def late_product(c):
        rows = pl.ds(c * CHUNK, CHUNK)
        for copy in late_loads[c]:
            copy.wait()
        total = product((2, 3, 4), rows, r_high[rows, :], r_low[rows, :])
        if c > 0:
            total = acc[...] + total
        if c < CHUNKS - 1:
            acc[...] = total
        else:
            h[2][...] = total[:W].reshape(2, 4, 16, 512)
            h[3][:, :, 0:16, :] = total[W : 2 * W].reshape(2, 4, 16, 512)
            h[3][:, :, 16:32, :] = total[2 * W :].reshape(2, 4, 16, 512)

    mine_rows = pl.ds(pl.multiple_of(mine * 16, 16), 16)
    pivots = [[] for _ in range(4)]
    others = [[] for _ in range(4)]
    nexts = [[] for _ in range(4)]
    rests = [[] for _ in range(4)]

    def send_pivot_rows(level):
        mat, gather = own[level], gat[level]
        for side, targets in ((1, far[level]), (0, near)):
            for to in targets:
                pivots[level].append(send(mat.at[0:16, 0:W], gather.at[side, mine_rows, 0:W], to))
        gather[0, mine_rows, 0:W] = mat[0:16, 0:W]

    def send_side_rows(level):
        for side, targets in ((1, far[level]), (0, near)):
            for to in targets:
                if level != 2 and to[3] == 1:
                    continue
                if level < 3:
                    copy = send(own[level].at[0:16, W:], gat[level].at[side, mine_rows, W:], to)
                else:
                    copy = send(own[3].at[16:32, :], gatx.at[side, mine_rows, :], to)
                others[level].append(copy)
        if level == 3:
            gatx[0, mine_rows, :] = own[3][16:32, :]
        else:
            gat[level][0, mine_rows, W:] = own[level][0:16, W:]

    first = [None] * 4
    second = [None] * 4

    def send_core(piece):
        low = W if piece == 0 else 0
        first[piece] = send(h[piece].at[1 - core, :, :, low:], rx1[piece], (z, x, 0, 1))

    def sum_cores(piece):
        receive([first[piece]])
        low = W if piece == 0 else 0
        half[piece][...] = h[piece][core, :, :, low:] + rx1[piece][...]

    def send_chips(piece):
        second[piece] = [
            send(half[piece].at[lax.rem(y + dy, 4)], rx2[piece].at[dy - 1], (z, x, dy, 0)) for dy in (2, 1, 3)
        ]

    def sum_chips(piece, rows):
        receive(second[piece])
        low = W if piece == 0 else 0
        own[0][rows, low:] = half[piece][y] + rx2[piece][0] + rx2[piece][1] + rx2[piece][2]

    direct = []
    for k, (_, _, dy, dc) in enumerate(near):
        piece = h[0].at[lax.rem(core + dc, 2), lax.rem(y + dy, 4), :, 0:W]
        direct.append(send(piece, rx0.at[k], (z, x, dy, dc)))
    send_core(0)
    send_core(1)
    late_product(0)
    for piece in (0, 1):
        sum_cores(piece)
        send_chips(piece)
    late_product(1)
    receive(direct)
    couplings = h[0][core, y, :, 0:W]
    for k in range(7):
        couplings = couplings + rx0[k]
    own[0][0:16, 0:W] = couplings
    send_pivot_rows(0)
    late_product(2)
    sum_chips(0, slice(0, 16))
    send_side_rows(0)
    late_product(3)
    send_core(2)
    send_core(3)
    sum_chips(1, slice(16, 32))
    nexts[0].append(send(own[0].at[16:32, :], rest[0].at[0:16, :], partners[0] + (0, 0)))
    for piece in (2, 3):
        sum_cores(piece)
        send_chips(piece)

    eye = jnp.where(
        lax.broadcasted_iota(jnp.int32, (W, W), 0) == lax.broadcasted_iota(jnp.int32, (W, W), 1), 1.0, 0.0
    )
    spread = [[] for _ in range(3)]

    def apply(targets, sources, weights, between):
        w_high, w_low = split(weights.T)
        size = 512
        for c in range(ROWS // size):
            if c == 3:
                between()
            rows = pl.ds(c * size, size)
            wide = [a_buf[i, rows, :] for i in sources]
            high, low = split(wide[0] if len(wide) == 1 else jnp.concatenate(wide, axis=1))
            change = one(high, w_high) + one(low, w_high) + one(high, w_low)
            for k, target in enumerate(targets):
                a_buf[target, rows, :] = a_buf[target, rows, :] - change[:, W * k : W * k + W]

    def blocks(level, b):
        return us[level][:, 16 * b : 16 * b + 16, :].reshape(W, W)

    core_rows = pl.ds(pl.multiple_of(core * 64, 64), 64)
    forward = [[], []]
    forward_late = [[], []]
    coef_forward = [[], [], []]

    def forward_side_rows(level):
        receive(others[level])
        both = gat[level].at[:, core_rows, W : 2 * W]
        forward[level].append(send(both, both, (z, x, 0, 1)))
        both = gat[level].at[:, core_rows, 2 * W :]
        forward_late[level].append(send(both, both, (z, x, 0, 1)))

    def forward_coefficients(level):
        receive(spread[level])
        half_of = us[level].at[pl.ds(core * 4, 4)]
        coef_forward[level].append(send(half_of, half_of, (z, x, 0, 1)))

    def send_partner(level, low, top, copies):
        target = rest[level].at[low - 16 : top - 16, :]
        copies[level].append(send(own[level].at[low:top, :], target, partners[level] + (0, 0)))

    def send_coefficients(level):
        for to in near:
            if to[3] == 1:
                continue
            spread[level].append(send(us[level].at[mine], us[level].at[mine], to))

    def advance(level, low, top, copies):
        receive(copies[level])
        gather, inv = gat[level], inv_buf[...]
        p_own, p_sib = gather[0, :, 0:W], gather[1, :, 0:W]
        w_own = own[level][low:top, 0:W]
        w_sib = rest[level][low - 16 : top - 16, 0:W]
        u_own = dot(w_sib - dot(w_own, p_sib, HIGH), inv, HIGH)
        u_sib = w_own - dot(u_own, p_own, HIGH)
        us[level][mine, low - 16 : top - 16, :] = u_own
        own[level + 1][low - 16 : top - 16, :] = (
            own[level][low:top, W:]
            + rest[level][low - 16 : top - 16, W:]
            - dot(u_own, gather[0, :, W:], HIGH)
            - dot(u_sib, gather[1, :, W:], HIGH)
        )

    def advance_pivots(level):
        receive(nexts[level])
        gather, inv = gat[level], inv_buf[...]
        p_own, p_sib = gather[0, :, 0:W], gather[1, :, 0:W]
        w_own = own[level][16:32, 0:W]
        u_own = dot(rest[level][0:16, 0:W] - dot(w_own, p_sib, HIGH), inv, HIGH)
        u_sib = w_own - dot(u_own, p_own, HIGH)
        us[level][mine, 0:16, :] = u_own

        def pass_on(low, top):
            own[level + 1][0:16, low - W : top - W] = (
                own[level][16:32, low:top]
                + rest[level][0:16, low:top]
                - dot(u_own, gather[0, :, low:top], HIGH)
                - dot(u_sib, gather[1, :, low:top], HIGH)
            )

        pass_on(W, 2 * W)
        send_pivot_rows(level + 1)
        if level < 2:
            receive(forward_late[level])
            pass_on(2 * W, (4 - level) * W)

    def solve_pivots(level, between=None):
        receive(pivots[level])
        return inverse(eye - dot(gat[level][0, :, 0:W], gat[level][1, :, 0:W]), between)

    mids = [[] for _ in range(4)]

    inv_buf[...] = solve_pivots(0, functools.partial(forward_side_rows, 0))
    receive(forward[0])
    advance_pivots(0)
    sum_chips(2, slice(32, 48))
    send_partner(0, 32, 48, mids)
    send_side_rows(1)
    sum_chips(3, slice(48, 80))
    send_partner(0, 48, 80, rests)
    advance(0, 32, 48, mids)
    send_partner(1, 16, 32, nexts)

    def late_rows():
        forward_side_rows(1)
        advance(0, 48, 80, rests)
        send_partner(1, 32, 64, rests)
        send_coefficients(0)

    inv = solve_pivots(1, late_rows)
    inv_buf[...] = inv
    receive(forward[1])
    advance_pivots(1)
    advance(1, 32, 64, rests)

    send_side_rows(2)
    send_partner(2, 16, 32, nexts)
    send_partner(2, 32, 48, rests)
    send_coefficients(1)
    forward_coefficients(0)
    inv_buf[...] = solve_pivots(2)
    receive(others[2])
    forward_coefficients(1)
    advance_pivots(2)
    advance(2, 32, 48, rests)

    receive(coef_forward[0] + coef_forward[1])
    def last_sends():
        send_side_rows(3)
        send_coefficients(2)

    u3 = jnp.concatenate([blocks(1, b) for b in range(3)], axis=0)
    u4 = jnp.concatenate([blocks(0, b) for b in range(1, 4)], axis=0) - dot(u3, blocks(0, 0))
    apply((2, 3, 4), (0, 1), jnp.concatenate([u4, u3], axis=1), last_sends)
    for copy in started[:-10]:
        copy.wait_send()
    del started[:-10]
    last_forward = []

    def forward_last():
        receive(others[3])
        both = gatx.at[:, core_rows, :]
        last_forward.append(send(both, both, (z, x, 0, 1)))
        forward_coefficients(2)

    inv = solve_pivots(3, forward_last)
    receive(last_forward)
    y_one = dot(gatx[1] - dot(gatx[0], gat[3][1]), inv)

    receive(coef_forward[2])
    y_two = blocks(2, 1) - dot(y_one, blocks(2, 0))
    w_high, w_low = split(jnp.concatenate([y_two.T, y_one.T], axis=0))
    w_both = jnp.concatenate([w_high, w_low], axis=1)
    size = ROWS // 8
    for c in range(8):
        rows = pl.ds(c * size, size)
        high, low = split(jnp.concatenate([a_buf[2, rows, :], a_buf[3, rows, :]], axis=1))
        both = one(high, w_both)
        out[rows, :] = a_buf[4, rows, :] - (both[:, :W] + both[:, W:] + one(low, w_high))
    for copy in started:
        copy.wait_send()


def body(l4, l3, l2, l1, r4, r3, r2, r1, x):
    f32 = jnp.float32
    hbm = pl.BlockSpec(memory_space=pl.ANY)
    pieces, widths = (16, 16, 16, 32), (384, 512, 512, 512)
    n_copies = 7 + 4 + 12 + 4 * 15 + 2 * 9 + 15 + 8 + 7 + 3 * 4
    return pl.pallas_call(
        solve_kernel,
        out_shape=jax.ShapeDtypeStruct((ROWS, W), f32),
        in_specs=[hbm] * 9,
        out_specs=pl.BlockSpec(memory_space=pltpu.VMEM),
        scratch_shapes=[
            pltpu.VMEM((5, ROWS, W), f32),
            pltpu.VMEM((4, ROWS, W), f32),
            pltpu.VMEM((ROWS, 512), jnp.bfloat16),
            pltpu.VMEM((ROWS, 512), jnp.bfloat16),
            pltpu.VMEM((384, 512), f32),
            [pltpu.VMEM((2, 4, n, 512), f32) for n in pieces],
            pltpu.VMEM((7, 16, W), f32),
            [pltpu.VMEM((4, n, lanes), f32) for n, lanes in zip(pieces, widths)],
            [pltpu.VMEM((4, n, lanes), f32) for n, lanes in zip(pieces, widths)],
            [pltpu.VMEM((3, n, lanes), f32) for n, lanes in zip(pieces, widths)],
            [pltpu.VMEM((16 * (5 - k), W * (4 - k)), f32) for k in range(4)],
            [pltpu.VMEM((16 * (4 - k), W * (4 - k)), f32) for k in range(3)],
            [pltpu.VMEM((2, W, W * (4 - k)), f32) for k in range(4)],
            pltpu.VMEM((2, W, W), f32),
            [pltpu.VMEM((8, 16 * (4 - k), W), f32) for k in range(3)],
            pltpu.VMEM((W, W), f32),
            pltpu.SemaphoreType.DMA((9, CHUNKS)),
            pltpu.SemaphoreType.DMA((2, n_copies)),
        ],
        compiler_params=pltpu.CompilerParams(
            collective_id=0, has_side_effects=True, vmem_limit_bytes=50 * 1024 * 1024
        ),
        name="solve",
    )(l4, l3, l2, l1, x, r4, r3, r2, r1)


def solution(mesh):
    spec = P(("outer", "inner"), None)
    return jax.shard_map(body, mesh=mesh, in_specs=(spec,) * 9, out_specs=spec, check_vma=False)
```
